32 devices in a mesh: grp: 2 (over y), ctx: 4 (over z), sub: 4 (over x, core).
Axes of the slice: x: 2, y: 2, z: 4, core: 2. Of those that a mesh axis runs over, the one named last changes fastest.
Arguments:
- query_rows: bfloat16 [8192, 1024], P(('grp', 'ctx', 'sub')), parts along dimension 0, may hold values from -6 to 6
- key_rows: bfloat16 [8192, 1024], P(('grp', 'ctx', 'sub')), parts along dimension 0, may hold values from -6 to 6
- value_rows: bfloat16 [8192, 1024], P(('grp', 'ctx', 'sub')), parts along dimension 0, may hold values from -6 to 6
- out_grad: bfloat16 [8192, 1024], P(('grp', 'ctx', 'sub')), parts along dimension 0, may hold values from -6 to 6
- reg_query: bfloat16 [6144, 1024], P(('grp', 'ctx', 'sub')), parts along dimension 0, may hold values from -6 to 6
- reg_out_grad: bfloat16 [6144, 1024], P(('grp', 'ctx', 'sub')), parts along dimension 0, may hold values from -6 to 6
- reg_offset: int32 [6144], P(('grp', 'ctx', 'sub')), parts along dimension 0, may hold values from 0 to 255
Outputs:
- grad_query: bfloat16 [8192, 1024], P(('grp', 'ctx', 'sub')), parts along dimension 0
- grad_key: bfloat16 [8192, 1024], P(('grp', 'ctx', 'sub')), parts along dimension 0
- grad_value: bfloat16 [8192, 1024], P(('grp', 'ctx', 'sub')), parts along dimension 0
- grad_reg_query: bfloat16 [6144, 1024], P(('grp', 'ctx', 'sub')), parts along dimension 0
The draws below stay inside these ranges and needn't reach their ends.
There are 2 independent parts, one for each index of `grp`. The reference program is written for one: setup_inputs(seed, part) draws one part's arguments, and reference() takes and returns one part's arrays. A program takes and returns all parts, laid end to end along the dimension named above; each array names one. Nothing has to cross between parts.
All inputs are finite; a program needn't handle non-finite values.
Results may differ from the reference program's by a relative error of at most 0.0049.
Values sent between devices are 32-bit elements; how exact they have to be, the bound alone decides.
A program may use at most 128 MiB of HBM per device.

```python
import jax
import jax.numpy as jnp
from jax import lax

HEADS = 8
HEAD = 128
TOK_DEV = 256
REG_DEV = 192
WIDTH = 1024
ROWS = 4096
REGS = 3072


def with_ends(values, key, smallest, top_value):
    index_at = [jax.random.randint(jax.random.fold_in(key, axis), (), 0, length) for axis, length in enumerate(values.shape)]
    widest = values.shape.index(max(values.shape))
    beside = index_at[:widest] + [(index_at[widest] + 1) % values.shape[widest]] + index_at[widest + 1:]
    return values.at[tuple(index_at)].set(smallest).at[tuple(beside)].set(top_value)


def steps_of(own_key, extent, cuts, low, top_value):
    gain = 1.0
    for position, shards_of in cuts:
        draws = jax.random.uniform(jax.random.fold_in(jax.random.fold_in(own_key, 6), position), (shards_of,), jnp.float32, low / len(cuts), top_value / len(cuts))
        gain = gain * jnp.repeat(jnp.exp(draws), extent[position] // shards_of).reshape((-1,) + (1,) * (len(extent) - 1 - position))
    return gain


def noise(key, shape, spread, bound, split=(), kind=jnp.bfloat16):
    level = steps_of(key, shape, split, -0.22, 0.18) if split else 1.0
    values = jax.random.normal(key, shape, jnp.float32) * spread * level
    return jnp.minimum(jnp.maximum(values, -bound), bound).astype(kind)


def setup_inputs(seed: int = 0, part: int = 0) -> dict:
    splits = jax.random.split(jax.random.key(seed), 8)
    part_splits = jax.random.split(jax.random.fold_in(splits[7], part), 8)
    return {
        "query_rows": noise(part_splits[0], (ROWS, WIDTH), 1.0, 6.0, ((0, 16),)),
        "key_rows": noise(part_splits[1], (ROWS, WIDTH), 1.0, 6.0, ((0, 16),)),
        "value_rows": noise(part_splits[2], (ROWS, WIDTH), 1.0, 6.0, ((0, 16),)),
        "out_grad": noise(part_splits[3], (ROWS, WIDTH), 1.0, 6.0, ((0, 16),)),
        "reg_query": noise(part_splits[4], (REGS, WIDTH), 1.0, 6.0, ((0, 16),)),
        "reg_out_grad": noise(part_splits[5], (REGS, WIDTH), 1.0, 6.0, ((0, 16),)),
        "reg_offset": with_ends(jax.random.randint(part_splits[6], (REGS,), 0, TOK_DEV), jax.random.fold_in(part_splits[6], 1), 0, TOK_DEV - 1).astype(jnp.int32),
    }


def reference(query_rows, key_rows, value_rows, out_grad, reg_query, reg_out_grad, reg_offset):
    blocks = ROWS // TOK_DEV

    def cut(array, count):
        return array.reshape(blocks, count, HEADS, HEAD)
    query_blocks = cut(query_rows, TOK_DEV)
    key_blocks = cut(key_rows, TOK_DEV)
    value_blocks = cut(value_rows, TOK_DEV)
    grad_blocks = cut(out_grad, TOK_DEV)
    regq_blocks = cut(reg_query, REG_DEV)
    regg_blocks = cut(reg_out_grad, REG_DEV)
    offset_blocks = reg_offset.reshape(blocks, REG_DEV)

    def local_states(items):
        query, key, value, grad, regq, regg = [a.astype(jnp.float32) for a in items]
        kv_state = jnp.einsum('shd,she->hde', key, value)
        grad_state = jnp.einsum('thd,the->hde', query, grad) + jnp.einsum('jhd,jhe->hde', regq, regg)
        return (kv_state, grad_state)
    kv_all, grad_all = lax.map(local_states, (query_blocks, key_blocks, value_blocks, grad_blocks, regq_blocks, regg_blocks))
    prefix = (jnp.cumsum(kv_all, axis=0) - kv_all).astype(jnp.bfloat16)
    suffix = (lax.optimization_barrier(jnp.sum(grad_all, axis=0)) - jnp.cumsum(grad_all, axis=0)).astype(jnp.bfloat16)
    factor = 1.0 / jnp.sqrt(jnp.float32(HEAD * ROWS))

    def block_grads(items):
        query, key, value, grad, regq, regg, offsets, before, after = items
        query, key, value, grad, regq, regg = [a.astype(jnp.float32) for a in (query, key, value, grad, regq, regg)]
        before = before.astype(jnp.float32)
        after = after.astype(jnp.float32)
        row_index = jnp.arange(TOK_DEV, dtype=jnp.int32)
        causal = row_index[:, None] >= row_index[None, :]
        reg_mask = offsets[:, None] >= row_index[None, :]
        zero = jnp.float32(0.0)
        out_scores = jnp.where(causal, jnp.einsum('the,she->hts', grad, value), zero).astype(jnp.bfloat16).astype(jnp.float32)
        qk_scores = jnp.where(causal, jnp.einsum('thd,shd->hts', query, key), zero).astype(jnp.bfloat16).astype(jnp.float32)
        reg_out_scores = jnp.where(reg_mask, jnp.einsum('jhe,she->hjs', regg, value), zero).astype(jnp.bfloat16).astype(jnp.float32)
        reg_qk_scores = jnp.where(reg_mask, jnp.einsum('jhd,shd->hjs', regq, key), zero).astype(jnp.bfloat16).astype(jnp.float32)
        grad_q = jnp.einsum('hts,shd->thd', out_scores, key) + jnp.einsum('the,hde->thd', grad, before)
        grad_rq = jnp.einsum('hjs,shd->jhd', reg_out_scores, key) + jnp.einsum('jhe,hde->jhd', regg, before)
        grad_k = jnp.einsum('hts,thd->shd', out_scores, query) + jnp.einsum('hjs,jhd->shd', reg_out_scores, regq) + jnp.einsum('she,hde->shd', value, after)
        grad_v = jnp.einsum('hts,the->she', qk_scores, grad) + jnp.einsum('hjs,jhe->she', reg_qk_scores, regg) + jnp.einsum('shd,hde->she', key, after)
        width = HEADS * HEAD
        return ((grad_q * factor).astype(jnp.bfloat16).reshape(TOK_DEV, width), (grad_k * factor).astype(jnp.bfloat16).reshape(TOK_DEV, width), (grad_v * factor).astype(jnp.bfloat16).reshape(TOK_DEV, width), (grad_rq * factor).astype(jnp.bfloat16).reshape(REG_DEV, width))
    grad_q, grad_k, grad_v, grad_rq = lax.map(block_grads, (query_blocks, key_blocks, value_blocks, grad_blocks, regq_blocks, regg_blocks, offset_blocks, prefix, suffix))
    width = HEADS * HEAD
    return (grad_q.reshape(ROWS, width), grad_k.reshape(ROWS, width), grad_v.reshape(ROWS, width), grad_rq.reshape(blocks * REG_DEV, width))
```

```python
import functools
import math

import jax
import jax.numpy as jnp
from jax import lax
from jax.experimental import pallas as pl
from jax.experimental.pallas import tpu as pltpu
from jax.sharding import PartitionSpec as P

HEADS = 8
HEAD = 128
MESH = pl.DeviceIdType.MESH


def carried_in(value, axis, join, neutral, backward):
    count, mine = (lax.axis_size(axis), lax.axis_index(axis))
    pieces = lax.all_gather(value, axis)
    if backward:
        pieces = pieces[::-1]
        mine = count - 1 - mine
    running = jnp.full_like(value, 0) + jnp.asarray(neutral, value.dtype)

    def hop(position, running):
        longer = join(running, pieces[position])
        return jnp.where(position < mine, longer, running)

    return lax.fori_loop(0, count - 1, hop, running)


def add_one(earlier, later):
    return earlier + later


def local(query_rows, key_rows, value_rows, out_grad, reg_query, reg_out_grad, reg_offset):
    row_count = query_rows.shape[0]
    reg_count = reg_query.shape[0]
    total_rows = row_count * lax.axis_size("ctx") * lax.axis_size("sub")
    factor = 1.0 / math.sqrt(HEAD * total_rows)
    query_heads = query_rows.reshape(row_count, HEADS, HEAD)
    key_heads = key_rows.reshape(row_count, HEADS, HEAD)
    value_heads = value_rows.reshape(row_count, HEADS, HEAD)
    grad_heads = out_grad.reshape(row_count, HEADS, HEAD)
    regq_heads = reg_query.reshape(reg_count, HEADS, HEAD)
    regg_heads = reg_out_grad.reshape(reg_count, HEADS, HEAD)
    kv_local = jnp.einsum(
        "shd,she->hde", key_heads, value_heads, preferred_element_type=jnp.float32
    )
    grad_local = jnp.einsum(
        "thd,the->hde", query_heads, grad_heads, preferred_element_type=jnp.float32
    ) + jnp.einsum("jhd,jhe->hde", regq_heads, regg_heads, preferred_element_type=jnp.float32)
    every_kv, every_grad = (
        lax.all_gather(kv_local[None], "sub", axis=0, tiled=True),
        lax.all_gather(grad_local[None], "sub", axis=0, tiled=True),
    )
    sub_count = lax.axis_size("sub")
    position = lax.axis_index("sub")
    slots = jnp.arange(sub_count, dtype=jnp.int32)
    earlier_mask = (slots < position)[:, None, None, None]
    later_mask = (slots > position)[:, None, None, None]
    zero_value = jnp.float32(0.0)
    inner_kv = jnp.sum(jnp.where(earlier_mask, every_kv, zero_value), axis=0)
    inner_grad = jnp.sum(jnp.where(later_mask, every_grad, zero_value), axis=0)
    share_rows = kv_local.shape[1] // sub_count
    start_row = position * share_rows
    share_kv = lax.dynamic_slice_in_dim(jnp.sum(every_kv, axis=0), start_row, share_rows, 1)
    share_grad = lax.dynamic_slice_in_dim(jnp.sum(every_grad, axis=0), start_row, share_rows, 1)
    share_zero = jnp.zeros_like(share_kv)
    outer_kv = carried_in(share_kv, "ctx", add_one, share_zero, False)
    outer_grad = carried_in(share_grad, "ctx", add_one, share_zero, True)
    full_kv, full_grad = (
        lax.all_gather(outer_kv, "sub", axis=1, tiled=True),
        lax.all_gather(outer_grad, "sub", axis=1, tiled=True),
    )
    before = (full_kv + inner_kv).astype(jnp.bfloat16)
    after = (full_grad + inner_grad).astype(jnp.bfloat16)
    row_index = jnp.arange(row_count, dtype=jnp.int32)
    causal = row_index[:, None] >= row_index[None, :]
    reg_mask = reg_offset[:, None] >= row_index[None, :]
    zero = jnp.float32(0.0)
    out_scores = jnp.where(
        causal,
        jnp.einsum("the,she->hts", grad_heads, value_heads, preferred_element_type=jnp.float32),
        zero,
    ).astype(jnp.bfloat16)
    qk_scores = jnp.where(
        causal,
        jnp.einsum("thd,shd->hts", query_heads, key_heads, preferred_element_type=jnp.float32),
        zero,
    ).astype(jnp.bfloat16)
    reg_out_scores = jnp.where(
        reg_mask,
        jnp.einsum("jhe,she->hjs", regg_heads, value_heads, preferred_element_type=jnp.float32),
        zero,
    ).astype(jnp.bfloat16)
    reg_qk_scores = jnp.where(
        reg_mask,
        jnp.einsum("jhd,shd->hjs", regq_heads, key_heads, preferred_element_type=jnp.float32),
        zero,
    ).astype(jnp.bfloat16)
    grad_q = jnp.einsum(
        "hts,shd->thd", out_scores, key_heads, preferred_element_type=jnp.float32
    ) + jnp.einsum("the,hde->thd", grad_heads, before, preferred_element_type=jnp.float32)
    grad_rq = jnp.einsum(
        "hjs,shd->jhd", reg_out_scores, key_heads, preferred_element_type=jnp.float32
    ) + jnp.einsum("jhe,hde->jhd", regg_heads, before, preferred_element_type=jnp.float32)
    grad_k = (
        jnp.einsum("hts,thd->shd", out_scores, query_heads, preferred_element_type=jnp.float32)
        + jnp.einsum("hjs,jhd->shd", reg_out_scores, regq_heads, preferred_element_type=jnp.float32)
        + jnp.einsum("she,hde->shd", value_heads, after, preferred_element_type=jnp.float32)
    )
    grad_v = (
        jnp.einsum("hts,the->she", qk_scores, grad_heads, preferred_element_type=jnp.float32)
        + jnp.einsum("hjs,jhe->she", reg_qk_scores, regg_heads, preferred_element_type=jnp.float32)
        + jnp.einsum("shd,hde->she", key_heads, after, preferred_element_type=jnp.float32)
    )
    width = HEADS * HEAD
    return (
        (grad_q * factor).astype(jnp.bfloat16).reshape(row_count, width),
        (grad_k * factor).astype(jnp.bfloat16).reshape(row_count, width),
        (grad_v * factor).astype(jnp.bfloat16).reshape(row_count, width),
        (grad_rq * factor).astype(jnp.bfloat16).reshape(reg_count, width),
    )


def contract(lhs, rhs, lhs_dim, rhs_dim):
    return lax.dot_general(
        lhs, rhs, (((lhs_dim,), (rhs_dim,)), ((), ())), preferred_element_type=jnp.float32
    )


def kernel(
    factor,
    q_hbm, k_hbm, v_hbm, g_hbm, rq_hbm, rg_hbm, off_ref,
    out_q, out_k, out_v, out_rq,
    qa, ga, ka, va, mine, pair, cross_out, cross_in, chain_in, chain_out, other, full, full16,
    acc_q, acc_k, acc_v,
    load_sem, pair_send, pair_recv, cross_send, cross_recv, chain_send, chain_recv,
    own_send, other_send, relay_send, full_recv,
):
    ctx_count, sub_count = lax.axis_size("ctx"), lax.axis_size("sub")
    each = HEADS // sub_count
    z, s = lax.axis_index("ctx"), lax.axis_index("sub")
    a, c = s // 2, s % 2
    partner = {"sub": 2 * a + 1 - c}
    across = {"sub": 2 * (1 - a) + c}
    rows, regs = ka.shape[0], rq_hbm.shape[0]

    loads = [
        pltpu.make_async_copy(k_hbm, ka, load_sem.at[0]),
        pltpu.make_async_copy(v_hbm, va, load_sem.at[1]),
        pltpu.make_async_copy(q_hbm, qa.at[pl.ds(0, rows)], load_sem.at[2]),
        pltpu.make_async_copy(g_hbm, ga.at[pl.ds(0, rows)], load_sem.at[3]),
        pltpu.make_async_copy(rq_hbm, qa.at[pl.ds(rows, regs)], load_sem.at[4]),
        pltpu.make_async_copy(rg_hbm, ga.at[pl.ds(rows, regs)], load_sem.at[5]),
    ]
    for load in loads:
        load.start()

    barrier = pltpu.get_barrier_semaphore()
    has_prev, has_next = z > 0, z < ctx_count - 1
    for target in (partner, across):
        pl.semaphore_signal(barrier, inc=1, device_id=target, device_id_type=MESH)

    @pl.when(has_prev)
    def _():
        pl.semaphore_signal(barrier, inc=1, device_id={"ctx": z - 1}, device_id_type=MESH)

    @pl.when(has_next)
    def _():
        pl.semaphore_signal(barrier, inc=1, device_id={"ctx": z + 1}, device_id_type=MESH)

    def cols(h):
        return pl.ds(pl.multiple_of(h * HEAD, HEAD), HEAD)

    def remote(src, dst, send, recv, target):
        return pltpu.make_async_remote_copy(
            src_ref=src, dst_ref=dst, send_sem=send, recv_sem=recv,
            device_id=target, device_id_type=MESH,
        )

    def pair_copy(k, h):
        return remote(mine.at[k, h], pair.at[k, h], pair_send.at[k, h], pair_recv.at[k, h], partner)

    def cross_copy(k, i):
        return remote(
            cross_out.at[k, i], cross_in.at[k, i], cross_send.at[k, i], cross_recv.at[k, i], across
        )

    def chain_copy(k, i, target):
        return remote(
            chain_out.at[k, i], chain_in.at[k, i], chain_send.at[k, i], chain_recv.at[k, i],
            {"ctx": target},
        )

    def own_copy(k, i):
        h = s * each + i
        return remote(full.at[k, h], full.at[k, h], own_send.at[k, i], full_recv.at[k, h], partner)

    def other_copy(k, i):
        return remote(
            other.at[k, i], full.at[k, s * each + i], other_send.at[k, i],
            full_recv.at[k, s * each + i], across,
        )

    def relay_copy(k, i):
        h = across["sub"] * each + i
        return remote(full.at[k, h], full.at[k, h], relay_send.at[k, i], full_recv.at[k, h], partner)

    first = jnp.where(2 * z >= ctx_count, 1, 0)
    kinds = (first, 1 - first)

    def state(h):
        mine[0, h] = contract(ka[:, cols(h)], va[:, cols(h)], 0, 0)
        mine[1, h] = contract(qa[:, cols(h)], ga[:, cols(h)], 0, 0)

    for load in loads:
        load.wait()
    greeted = 2 + jnp.where(has_prev, 1, 0) + jnp.where(has_next, 1, 0)

    for i in range(each):
        state((2 * (1 - a) + 1 - c) * each + i)
    pl.semaphore_wait(barrier, greeted)
    for i in range(each):
        for k in kinds:
            pair_copy(k, (2 * (1 - a) + 1 - c) * each + i).start()
    for i in range(each):
        state(across["sub"] * each + i)
    for i in range(each):
        state((2 * a + 1 - c) * each + i)
    for i in range(each):
        for k in kinds:
            pair_copy(k, (2 * a + 1 - c) * each + i).start()

    for k in kinds:
        for i in range(each):
            h = across["sub"] * each + i
            pair_copy(k, h).wait_recv()
            cross_out[k, i] = mine[k, h] + pair[k, h]
    for k in kinds:
        for i in range(each):
            cross_copy(k, i).start()
    for i in range(each):
        state(s * each + i)
    for side in range(2):
        for i in range(each):
            pair_copy(c, (2 * side + c) * each + i).start()

    place = lax.broadcasted_iota(jnp.int32, (rows, rows), 0)
    time = lax.broadcasted_iota(jnp.int32, (rows, rows), 1)
    reg_place = lax.broadcasted_iota(jnp.int32, (rows, regs), 0)

    def masked(scores):
        zero = jnp.float32(0.0)
        regular = jnp.where(time >= place, scores[:, :rows], zero)
        register = jnp.where(off_ref[...] >= reg_place, scores[:, rows:], zero)
        return jnp.concatenate([regular, register], axis=1).astype(jnp.bfloat16)

    def scores(h):
        at = cols(h)
        key, value, query, grad = ka[:, at], va[:, at], qa[:, at], ga[:, at]
        out_scores = masked(contract(value, grad, 1, 1))
        qk_scores = masked(contract(key, query, 1, 1))
        acc_q[:, at] = contract(out_scores, key, 0, 0)
        acc_k[:, at] = contract(out_scores, query, 1, 0)
        acc_v[:, at] = contract(qk_scores, grad, 1, 0)

    def some_scores(low, high):
        lax.fori_loop(low, high, lambda h, _: (scores(h), 0)[1], 0)

    def chain(k):
        has_in = jnp.where(k == 0, has_prev, has_next)
        has_out = jnp.where(k == 0, has_next, has_prev)
        target = jnp.where(k == 0, z + 1, z - 1)
        ahead = a == k
        for i in range(each):
            h = s * each + i
            pair_copy(k, h).wait_recv()
            cross_copy(k, i).wait_recv()

            @pl.when(has_in)
            def _():
                chain_copy(k, i, target).wait_recv()

            @pl.when(jnp.logical_not(has_in))
            def _():
                chain_in[k, i] = jnp.zeros((HEAD, HEAD), jnp.float32)

            @pl.when(has_out)
            def _():
                chain_out[k, i] = (chain_in[k, i] + (mine[k, h] + pair[k, h])) + cross_in[k, i]
                chain_copy(k, i, target).start()

            carried = chain_in[k, i]
            zero = jnp.float32(0.0)
            own = mine[k, h] + pair[k, h]
            other[k, i] = carried + jnp.where(ahead, own, zero)
            other_copy(k, i).start()
            full[k, h] = carried + jnp.where(ahead, zero, cross_in[k, i])
            own_copy(k, i).start()

    some_scores(0, 3)
    chain(kinds[0])
    some_scores(3, 6)
    chain(kinds[1])
    some_scores(6, HEADS)

    for k in kinds:
        for i in range(each):
            other_copy_in = remote(
                other.at[k, i], full.at[k, across["sub"] * each + i], other_send.at[k, i],
                full_recv.at[k, across["sub"] * each + i], across,
            )
            other_copy_in.wait_recv()
            relay_copy(k, i).start()

    def full_wait(k, h):
        remote(full.at[k, h], full.at[k, h], own_send.at[0, 0], full_recv.at[k, h], partner).wait_recv()

    for side in range(2):
        for i in range(each):
            pair_copy(1 - c, (2 * side + 1 - c) * each + i).wait_recv()

    def finish(h):
        at = cols(h)
        full16[1 - c, h] = (full[1 - c, h] + pair[1 - c, h]).astype(jnp.bfloat16)
        full16[c, h] = full[c, h].astype(jnp.bfloat16)
        before, after = full16[0, h], full16[1, h]
        whole = (acc_q[:, at] + contract(ga[:, at], before, 1, 1)) * factor
        out_q[:, at] = whole[:rows].astype(jnp.bfloat16)
        out_rq[:, at] = whole[rows:].astype(jnp.bfloat16)
        out_k[:, at] = ((acc_k[:, at] + contract(va[:, at], after, 1, 1)) * factor).astype(jnp.bfloat16)
        out_v[:, at] = ((acc_v[:, at] + contract(ka[:, at], after, 1, 0)) * factor).astype(jnp.bfloat16)

    for i in range(each):
        finish(s * each + i)
    for i in range(each):
        finish(across["sub"] * each + i)
    for i in range(each):
        h = (2 * a + 1 - c) * each + i
        full_wait(0, h)
        full_wait(1, h)
        finish(h)
    for i in range(each):
        h = (2 * (1 - a) + 1 - c) * each + i
        full_wait(0, h)
        full_wait(1, h)
        finish(h)

    for k in range(2):
        for i in range(each):
            for side in range(2):
                pair_copy(k, (2 * side + 1 - c) * each + i).wait_send()
            cross_copy(k, i).wait_send()
            other_copy(k, i).wait_send()
            own_copy(k, i).wait_send()
            relay_copy(k, i).wait_send()

            @pl.when((has_next, has_prev)[k])
            def _():
                chain_copy(k, i, (z + 1, z - 1)[k]).wait_send()
    for side in range(2):
        for i in range(each):
            pair_copy(c, (2 * side + c) * each + i).wait_send()


def fused(query_rows, key_rows, value_rows, out_grad, reg_query, reg_out_grad, reg_offset):
    rows, width = query_rows.shape
    regs = reg_query.shape[0]
    sub_count = lax.axis_size("sub")
    factor = 1.0 / math.sqrt(HEAD * rows * lax.axis_size("ctx") * sub_count)
    each = HEADS // sub_count
    all_states = pltpu.VMEM((2, HEADS, HEAD, HEAD), jnp.float32)
    few_states = pltpu.VMEM((2, each, HEAD, HEAD), jnp.float32)
    all_sems = pltpu.SemaphoreType.DMA((2, HEADS))
    few_sems = pltpu.SemaphoreType.DMA((2, each))
    vmem = pl.BlockSpec(memory_space=pltpu.VMEM)
    out_q, out_k, out_v, out_rq = pl.pallas_call(
        functools.partial(kernel, factor),
        out_shape=(
            jax.ShapeDtypeStruct((rows, width), jnp.bfloat16),
            jax.ShapeDtypeStruct((rows, width), jnp.bfloat16),
            jax.ShapeDtypeStruct((rows, width), jnp.bfloat16),
            jax.ShapeDtypeStruct((regs, width), jnp.bfloat16),
        ),
        in_specs=[pl.BlockSpec(memory_space=pl.ANY)] * 6 + [vmem],
        out_specs=(vmem,) * 4,
        scratch_shapes=[
            pltpu.VMEM((rows + regs, width), jnp.bfloat16),
            pltpu.VMEM((rows + regs, width), jnp.bfloat16),
            pltpu.VMEM((rows, width), jnp.bfloat16),
            pltpu.VMEM((rows, width), jnp.bfloat16),
            all_states, all_states,
            few_states, few_states, few_states, few_states, few_states,
            all_states,
            pltpu.VMEM((2, HEADS, HEAD, HEAD), jnp.bfloat16),
            pltpu.VMEM((rows + regs, width), jnp.float32),
            pltpu.VMEM((rows, width), jnp.float32),
            pltpu.VMEM((rows, width), jnp.float32),
            pltpu.SemaphoreType.DMA((6,)),
            all_sems, all_sems,
            few_sems, few_sems, few_sems, few_sems,
            few_sems, few_sems, few_sems, all_sems,
        ],
        compiler_params=pltpu.CompilerParams(
            collective_id=0, has_side_effects=True, vmem_limit_bytes=40 * 1024 * 1024
        ),
    )(
        query_rows, key_rows, value_rows, out_grad, reg_query, reg_out_grad,
        reg_offset.reshape(1, regs),
    )
    return out_q, out_k, out_v, out_rq


def solution(mesh):
    placed = (
        P(("grp", "ctx", "sub"), None),
        P(("grp", "ctx", "sub"), None),
        P(("grp", "ctx", "sub"), None),
        P(("grp", "ctx", "sub"), None),
        P(("grp", "ctx", "sub"), None),
        P(("grp", "ctx", "sub"), None),
        P(("grp", "ctx", "sub")),
    )
    return jax.shard_map(
        fused if mesh.shape["sub"] == 4 else local,
        mesh=mesh,
        in_specs=placed,
        out_specs=(
            P(("grp", "ctx", "sub"), None),
            P(("grp", "ctx", "sub"), None),
            P(("grp", "ctx", "sub"), None),
            P(("grp", "ctx", "sub"), None),
        ),
        check_vma=False,
    )
```

```python
import functools
import math

import jax
import jax.numpy as jnp
from jax import lax
from jax.experimental import pallas as pl
from jax.experimental.pallas import tpu as pltpu
from jax.sharding import PartitionSpec as P

HEADS = 8
HEAD = 128
MESH = pl.DeviceIdType.MESH


def carried_in(value, axis, join, neutral, backward):
    count, mine = (lax.axis_size(axis), lax.axis_index(axis))
    pieces = lax.all_gather(value, axis)
    if backward:
        pieces = pieces[::-1]
        mine = count - 1 - mine
    running = jnp.full_like(value, 0) + jnp.asarray(neutral, value.dtype)

    def hop(position, running):
        longer = join(running, pieces[position])
        return jnp.where(position < mine, longer, running)

    return lax.fori_loop(0, count - 1, hop, running)


def add_one(earlier, later):
    return earlier + later


def local(query_rows, key_rows, value_rows, out_grad, reg_query, reg_out_grad, reg_offset):
    row_count = query_rows.shape[0]
    reg_count = reg_query.shape[0]
    total_rows = row_count * lax.axis_size("ctx") * lax.axis_size("sub")
    factor = 1.0 / math.sqrt(HEAD * total_rows)
    query_heads = query_rows.reshape(row_count, HEADS, HEAD)
    key_heads = key_rows.reshape(row_count, HEADS, HEAD)
    value_heads = value_rows.reshape(row_count, HEADS, HEAD)
    grad_heads = out_grad.reshape(row_count, HEADS, HEAD)
    regq_heads = reg_query.reshape(reg_count, HEADS, HEAD)
    regg_heads = reg_out_grad.reshape(reg_count, HEADS, HEAD)
    kv_local = jnp.einsum(
        "shd,she->hde", key_heads, value_heads, preferred_element_type=jnp.float32
    )
    grad_local = jnp.einsum(
        "thd,the->hde", query_heads, grad_heads, preferred_element_type=jnp.float32
    ) + jnp.einsum("jhd,jhe->hde", regq_heads, regg_heads, preferred_element_type=jnp.float32)
    every_kv, every_grad = (
        lax.all_gather(kv_local[None], "sub", axis=0, tiled=True),
        lax.all_gather(grad_local[None], "sub", axis=0, tiled=True),
    )
    sub_count = lax.axis_size("sub")
    position = lax.axis_index("sub")
    slots = jnp.arange(sub_count, dtype=jnp.int32)
    earlier_mask = (slots < position)[:, None, None, None]
    later_mask = (slots > position)[:, None, None, None]
    zero_value = jnp.float32(0.0)
    inner_kv = jnp.sum(jnp.where(earlier_mask, every_kv, zero_value), axis=0)
    inner_grad = jnp.sum(jnp.where(later_mask, every_grad, zero_value), axis=0)
    share_rows = kv_local.shape[1] // sub_count
    start_row = position * share_rows
    share_kv = lax.dynamic_slice_in_dim(jnp.sum(every_kv, axis=0), start_row, share_rows, 1)
    share_grad = lax.dynamic_slice_in_dim(jnp.sum(every_grad, axis=0), start_row, share_rows, 1)
    share_zero = jnp.zeros_like(share_kv)
    outer_kv = carried_in(share_kv, "ctx", add_one, share_zero, False)
    outer_grad = carried_in(share_grad, "ctx", add_one, share_zero, True)
    full_kv, full_grad = (
        lax.all_gather(outer_kv, "sub", axis=1, tiled=True),
        lax.all_gather(outer_grad, "sub", axis=1, tiled=True),
    )
    before = (full_kv + inner_kv).astype(jnp.bfloat16)
    after = (full_grad + inner_grad).astype(jnp.bfloat16)
    row_index = jnp.arange(row_count, dtype=jnp.int32)
    causal = row_index[:, None] >= row_index[None, :]
    reg_mask = reg_offset[:, None] >= row_index[None, :]
    zero = jnp.float32(0.0)
    out_scores = jnp.where(
        causal,
        jnp.einsum("the,she->hts", grad_heads, value_heads, preferred_element_type=jnp.float32),
        zero,
    ).astype(jnp.bfloat16)
    qk_scores = jnp.where(
        causal,
        jnp.einsum("thd,shd->hts", query_heads, key_heads, preferred_element_type=jnp.float32),
        zero,
    ).astype(jnp.bfloat16)
    reg_out_scores = jnp.where(
        reg_mask,
        jnp.einsum("jhe,she->hjs", regg_heads, value_heads, preferred_element_type=jnp.float32),
        zero,
    ).astype(jnp.bfloat16)
    reg_qk_scores = jnp.where(
        reg_mask,
        jnp.einsum("jhd,shd->hjs", regq_heads, key_heads, preferred_element_type=jnp.float32),
        zero,
    ).astype(jnp.bfloat16)
    grad_q = jnp.einsum(
        "hts,shd->thd", out_scores, key_heads, preferred_element_type=jnp.float32
    ) + jnp.einsum("the,hde->thd", grad_heads, before, preferred_element_type=jnp.float32)
    grad_rq = jnp.einsum(
        "hjs,shd->jhd", reg_out_scores, key_heads, preferred_element_type=jnp.float32
    ) + jnp.einsum("jhe,hde->jhd", regg_heads, before, preferred_element_type=jnp.float32)
    grad_k = (
        jnp.einsum("hts,thd->shd", out_scores, query_heads, preferred_element_type=jnp.float32)
        + jnp.einsum("hjs,jhd->shd", reg_out_scores, regq_heads, preferred_element_type=jnp.float32)
        + jnp.einsum("she,hde->shd", value_heads, after, preferred_element_type=jnp.float32)
    )
    grad_v = (
        jnp.einsum("hts,the->she", qk_scores, grad_heads, preferred_element_type=jnp.float32)
        + jnp.einsum("hjs,jhe->she", reg_qk_scores, regg_heads, preferred_element_type=jnp.float32)
        + jnp.einsum("shd,hde->she", key_heads, after, preferred_element_type=jnp.float32)
    )
    width = HEADS * HEAD
    return (
        (grad_q * factor).astype(jnp.bfloat16).reshape(row_count, width),
        (grad_k * factor).astype(jnp.bfloat16).reshape(row_count, width),
        (grad_v * factor).astype(jnp.bfloat16).reshape(row_count, width),
        (grad_rq * factor).astype(jnp.bfloat16).reshape(reg_count, width),
    )


def contract(lhs, rhs, lhs_dim, rhs_dim):
    return lax.dot_general(
        lhs, rhs, (((lhs_dim,), (rhs_dim,)), ((), ())), preferred_element_type=jnp.float32
    )


def kernel(
    factor,
    q_hbm, k_hbm, v_hbm, g_hbm, rq_hbm, rg_hbm, off_ref,
    out_q, out_k, out_v, out_rq,
    qa, ga, ka, va, mine, pair, cross_out, cross_in, chain_in, chain_out, other, full, full16,
    acc_q, acc_k, acc_v,
    load_sem, pair_send, pair_recv, cross_send, cross_recv, chain_send, chain_recv,
    own_send, other_send, relay_send, full_recv,
):
    ctx_count, sub_count = lax.axis_size("ctx"), lax.axis_size("sub")
    each = HEADS // sub_count
    z, s = lax.axis_index("ctx"), lax.axis_index("sub")
    a, c = s // 2, s % 2
    partner = {"sub": 2 * a + 1 - c}
    across = {"sub": 2 * (1 - a) + c}
    rows, regs = ka.shape[0], rq_hbm.shape[0]

    loads = [
        pltpu.make_async_copy(k_hbm, ka, load_sem.at[0]),
        pltpu.make_async_copy(v_hbm, va, load_sem.at[1]),
        pltpu.make_async_copy(q_hbm, qa.at[pl.ds(0, rows)], load_sem.at[2]),
        pltpu.make_async_copy(g_hbm, ga.at[pl.ds(0, rows)], load_sem.at[3]),
        pltpu.make_async_copy(rq_hbm, qa.at[pl.ds(rows, regs)], load_sem.at[4]),
        pltpu.make_async_copy(rg_hbm, ga.at[pl.ds(rows, regs)], load_sem.at[5]),
    ]
    for load in loads:
        load.start()

    barrier = pltpu.get_barrier_semaphore()
    has_prev, has_next = z > 0, z < ctx_count - 1
    for target in (partner, across):
        pl.semaphore_signal(barrier, inc=1, device_id=target, device_id_type=MESH)

    @pl.when(has_prev)
    def _():
        pl.semaphore_signal(barrier, inc=1, device_id={"ctx": z - 1}, device_id_type=MESH)

    @pl.when(has_next)
    def _():
        pl.semaphore_signal(barrier, inc=1, device_id={"ctx": z + 1}, device_id_type=MESH)

    def cols(h):
        return pl.ds(pl.multiple_of(h * HEAD, HEAD), HEAD)

    def remote(src, dst, send, recv, target):
        return pltpu.make_async_remote_copy(
            src_ref=src, dst_ref=dst, send_sem=send, recv_sem=recv,
            device_id=target, device_id_type=MESH,
        )

    def pair_copy(k, h):
        return remote(mine.at[k, h], pair.at[k, h], pair_send.at[k, h], pair_recv.at[k, h], partner)

    def cross_copy(k, i):
        return remote(
            cross_out.at[k, i], cross_in.at[k, i], cross_send.at[k, i], cross_recv.at[k, i], across
        )

    def chain_copy(k, i, target):
        return remote(
            chain_out.at[k, i], chain_in.at[k, i], chain_send.at[k, i], chain_recv.at[k, i],
            {"ctx": target},
        )

    def own_copy(k, i):
        h = s * each + i
        return remote(full.at[k, h], full.at[k, h], own_send.at[k, i], full_recv.at[k, h], partner)

    def other_copy(k, i):
        return remote(
            other.at[k, i], full.at[k, s * each + i], other_send.at[k, i],
            full_recv.at[k, s * each + i], across,
        )

    def relay_copy(k, i):
        h = across["sub"] * each + i
        return remote(full.at[k, h], full.at[k, h], relay_send.at[k, i], full_recv.at[k, h], partner)

    first = jnp.where(2 * z >= ctx_count, 1, 0)
    kinds = (first, 1 - first)

    def state(h):
        mine[0, h] = contract(ka[:, cols(h)], va[:, cols(h)], 0, 0)
        mine[1, h] = contract(qa[:, cols(h)], ga[:, cols(h)], 0, 0)

    for load in loads:
        load.wait()
    greeted = 2 + jnp.where(has_prev, 1, 0) + jnp.where(has_next, 1, 0)

    for i in range(each):
        state((2 * (1 - a) + 1 - c) * each + i)
    pl.semaphore_wait(barrier, greeted)
    for i in range(each):
        for k in kinds:
            pair_copy(k, (2 * (1 - a) + 1 - c) * each + i).start()
    for i in range(each):
        state(across["sub"] * each + i)
    for i in range(each):
        state((2 * a + 1 - c) * each + i)
    for i in range(each):
        for k in kinds:
            pair_copy(k, (2 * a + 1 - c) * each + i).start()

    for k in kinds:
        for i in range(each):
            h = across["sub"] * each + i
            pair_copy(k, h).wait_recv()
            cross_out[k, i] = mine[k, h] + pair[k, h]
    for k in kinds:
        for i in range(each):
            cross_copy(k, i).start()
    for i in range(each):
        state(s * each + i)
    for side in range(2):
        for i in range(each):
            pair_copy(c, (2 * side + c) * each + i).start()

    place = lax.broadcasted_iota(jnp.int32, (rows, rows), 0)
    time = lax.broadcasted_iota(jnp.int32, (rows, rows), 1)
    reg_place = lax.broadcasted_iota(jnp.int32, (rows, regs), 0)

    def masked(scores):
        zero = jnp.float32(0.0)
        regular = jnp.where(time >= place, scores[:, :rows], zero)
        register = jnp.where(off_ref[...] >= reg_place, scores[:, rows:], zero)
        return jnp.concatenate([regular, register], axis=1).astype(jnp.bfloat16)

    def scores(h):
        at = cols(h)
        key, value, query, grad = ka[:, at], va[:, at], qa[:, at], ga[:, at]
        out_scores = masked(contract(value, grad, 1, 1))
        qk_scores = masked(contract(key, query, 1, 1))
        acc_q[:, at] = contract(out_scores, key, 0, 0)
        acc_k[:, at] = contract(out_scores, query, 1, 0)
        acc_v[:, at] = contract(qk_scores, grad, 1, 0)

    def some_scores(low, high):
        lax.fori_loop(low, high, lambda h, _: (scores(h), 0)[1], 0)

    def chain(k):
        has_in = jnp.where(k == 0, has_prev, has_next)
        has_out = jnp.where(k == 0, has_next, has_prev)
        target = jnp.where(k == 0, z + 1, z - 1)
        ahead = a == k
        for i in range(each):
            h = s * each + i
            pair_copy(k, h).wait_recv()
            cross_copy(k, i).wait_recv()

            @pl.when(has_in)
            def _():
                chain_copy(k, i, target).wait_recv()

            @pl.when(jnp.logical_not(has_in))
            def _():
                chain_in[k, i] = jnp.zeros((HEAD, HEAD), jnp.float32)

            @pl.when(has_out)
            def _():
                chain_out[k, i] = (chain_in[k, i] + (mine[k, h] + pair[k, h])) + cross_in[k, i]
                chain_copy(k, i, target).start()

            carried = chain_in[k, i]
            zero = jnp.float32(0.0)
            own = mine[k, h] + pair[k, h]
            other[k, i] = carried + jnp.where(ahead, own, zero)
            other_copy(k, i).start()
            full[k, h] = carried + jnp.where(ahead, zero, cross_in[k, i])
            own_copy(k, i).start()

    some_scores(0, 3)
    chain(kinds[0])
    some_scores(3, 6)
    chain(kinds[1])
    some_scores(6, HEADS)

    for k in kinds:
        for i in range(each):
            other_copy_in = remote(
                other.at[k, i], full.at[k, across["sub"] * each + i], other_send.at[k, i],
                full_recv.at[k, across["sub"] * each + i], across,
            )
            other_copy_in.wait_recv()
            relay_copy(k, i).start()

    def full_wait(k, h):
        remote(full.at[k, h], full.at[k, h], own_send.at[0, 0], full_recv.at[k, h], partner).wait_recv()

    for side in range(2):
        for i in range(each):
            pair_copy(1 - c, (2 * side + 1 - c) * each + i).wait_recv()

    def finish(h):
        at = cols(h)
        full16[1 - c, h] = (full[1 - c, h] + pair[1 - c, h]).astype(jnp.bfloat16)
        full16[c, h] = full[c, h].astype(jnp.bfloat16)
        before, after = full16[0, h], full16[1, h]
        whole = (acc_q[:, at] + contract(ga[:, at], before, 1, 1)) * factor
        out_q[:, at] = whole[:rows].astype(jnp.bfloat16)
        out_rq[:, at] = whole[rows:].astype(jnp.bfloat16)
        out_k[:, at] = ((acc_k[:, at] + contract(va[:, at], after, 1, 1)) * factor).astype(jnp.bfloat16)
        out_v[:, at] = ((acc_v[:, at] + contract(ka[:, at], after, 1, 0)) * factor).astype(jnp.bfloat16)

    for i in range(each):
        finish(s * each + i)
    for i in range(each):
        finish(across["sub"] * each + i)
    for i in range(each):
        h = (2 * a + 1 - c) * each + i
        full_wait(0, h)
        full_wait(1, h)
        finish(h)
    for i in range(each):
        h = (2 * (1 - a) + 1 - c) * each + i
        full_wait(0, h)
        full_wait(1, h)
        finish(h)

    for k in range(2):
        for i in range(each):
            for side in range(2):
                pair_copy(k, (2 * side + 1 - c) * each + i).wait_send()
            cross_copy(k, i).wait_send()
            other_copy(k, i).wait_send()
            own_copy(k, i).wait_send()
            relay_copy(k, i).wait_send()

            @pl.when((has_next, has_prev)[k])
            def _():
                chain_copy(k, i, (z + 1, z - 1)[k]).wait_send()
    for side in range(2):
        for i in range(each):
            pair_copy(c, (2 * side + c) * each + i).wait_send()


def store_all(*refs):
    sources, results, held, in_sem, out_sem = refs[:4], refs[4:8], refs[8:12], refs[12], refs[13]
    loads = [pltpu.make_async_copy(sources[i], held[i], in_sem.at[i]) for i in range(4)]
    stores = [pltpu.make_async_copy(held[i], results[i], out_sem.at[i]) for i in range(4)]
    for load in loads:
        load.start()
    for load, store in zip(loads, stores):
        load.wait()
        store.start()
    for store in stores:
        store.wait()


def fused(query_rows, key_rows, value_rows, out_grad, reg_query, reg_out_grad, reg_offset):
    rows, width = query_rows.shape
    regs = reg_query.shape[0]
    sub_count = lax.axis_size("sub")
    factor = 1.0 / math.sqrt(HEAD * rows * lax.axis_size("ctx") * sub_count)
    each = HEADS // sub_count
    all_states = pltpu.VMEM((2, HEADS, HEAD, HEAD), jnp.float32)
    few_states = pltpu.VMEM((2, each, HEAD, HEAD), jnp.float32)
    all_sems = pltpu.SemaphoreType.DMA((2, HEADS))
    few_sems = pltpu.SemaphoreType.DMA((2, each))
    vmem = pl.BlockSpec(memory_space=pltpu.VMEM)
    hbm = pl.BlockSpec(memory_space=pltpu.HBM)
    shapes = (
        jax.ShapeDtypeStruct((rows, width), jnp.bfloat16),
        jax.ShapeDtypeStruct((rows, width), jnp.bfloat16),
        jax.ShapeDtypeStruct((rows, width), jnp.bfloat16),
        jax.ShapeDtypeStruct((regs, width), jnp.bfloat16),
    )
    results = pl.pallas_call(
        functools.partial(kernel, factor),
        out_shape=shapes,
        in_specs=[hbm] * 6 + [vmem],
        out_specs=(vmem,) * 4,
        scratch_shapes=[
            pltpu.VMEM((rows + regs, width), jnp.bfloat16),
            pltpu.VMEM((rows + regs, width), jnp.bfloat16),
            pltpu.VMEM((rows, width), jnp.bfloat16),
            pltpu.VMEM((rows, width), jnp.bfloat16),
            all_states, all_states,
            few_states, few_states, few_states, few_states, few_states,
            all_states,
            pltpu.VMEM((2, HEADS, HEAD, HEAD), jnp.bfloat16),
            pltpu.VMEM((rows + regs, width), jnp.float32),
            pltpu.VMEM((rows, width), jnp.float32),
            pltpu.VMEM((rows, width), jnp.float32),
            pltpu.SemaphoreType.DMA((6,)),
            all_sems, all_sems,
            few_sems, few_sems, few_sems, few_sems,
            few_sems, few_sems, few_sems, all_sems,
        ],
        compiler_params=pltpu.CompilerParams(
            collective_id=0, has_side_effects=True, vmem_limit_bytes=63400 * 1024
        ),
    )(
        query_rows, key_rows, value_rows, out_grad, reg_query, reg_out_grad,
        reg_offset.reshape(1, regs),
    )
    return pl.pallas_call(
        store_all,
        out_shape=shapes,
        in_specs=[hbm] * 4,
        out_specs=(hbm,) * 4,
        scratch_shapes=[pltpu.VMEM(shape.shape, shape.dtype) for shape in shapes]
        + [pltpu.SemaphoreType.DMA((4,)), pltpu.SemaphoreType.DMA((4,))],
        compiler_params=pltpu.CompilerParams(vmem_limit_bytes=63400 * 1024),
    )(*results)


def solution(mesh):
    placed = (
        P(("grp", "ctx", "sub"), None),
        P(("grp", "ctx", "sub"), None),
        P(("grp", "ctx", "sub"), None),
        P(("grp", "ctx", "sub"), None),
        P(("grp", "ctx", "sub"), None),
        P(("grp", "ctx", "sub"), None),
        P(("grp", "ctx", "sub")),
    )
    return jax.shard_map(
        fused if mesh.shape["sub"] == 4 else local,
        mesh=mesh,
        in_specs=placed,
        out_specs=(
            P(("grp", "ctx", "sub"), None),
            P(("grp", "ctx", "sub"), None),
            P(("grp", "ctx", "sub"), None),
            P(("grp", "ctx", "sub"), None),
        ),
        check_vma=False,
    )
```

```python
import functools
import math

import jax
import jax.numpy as jnp
from jax import lax
from jax.experimental import pallas as pl
from jax.experimental.pallas import tpu as pltpu
from jax.sharding import PartitionSpec as P

HEADS = 8
HEAD = 128
MESH = pl.DeviceIdType.MESH
PARTS = 2


def carried_in(value, axis, join, neutral, backward):
    count, mine = (lax.axis_size(axis), lax.axis_index(axis))
    pieces = lax.all_gather(value, axis)
    if backward:
        pieces = pieces[::-1]
        mine = count - 1 - mine
    running = jnp.full_like(value, 0) + jnp.asarray(neutral, value.dtype)

    def hop(position, running):
        longer = join(running, pieces[position])
        return jnp.where(position < mine, longer, running)

    return lax.fori_loop(0, count - 1, hop, running)


def add_one(earlier, later):
    return earlier + later


def local(query_rows, key_rows, value_rows, out_grad, reg_query, reg_out_grad, reg_offset):
    row_count = query_rows.shape[0]
    reg_count = reg_query.shape[0]
    total_rows = row_count * lax.axis_size("ctx") * lax.axis_size("sub")
    factor = 1.0 / math.sqrt(HEAD * total_rows)
    query_heads = query_rows.reshape(row_count, HEADS, HEAD)
    key_heads = key_rows.reshape(row_count, HEADS, HEAD)
    value_heads = value_rows.reshape(row_count, HEADS, HEAD)
    grad_heads = out_grad.reshape(row_count, HEADS, HEAD)
    regq_heads = reg_query.reshape(reg_count, HEADS, HEAD)
    regg_heads = reg_out_grad.reshape(reg_count, HEADS, HEAD)
    kv_local = jnp.einsum(
        "shd,she->hde", key_heads, value_heads, preferred_element_type=jnp.float32
    )
    grad_local = jnp.einsum(
        "thd,the->hde", query_heads, grad_heads, preferred_element_type=jnp.float32
    ) + jnp.einsum("jhd,jhe->hde", regq_heads, regg_heads, preferred_element_type=jnp.float32)
    every_kv, every_grad = (
        lax.all_gather(kv_local[None], "sub", axis=0, tiled=True),
        lax.all_gather(grad_local[None], "sub", axis=0, tiled=True),
    )
    sub_count = lax.axis_size("sub")
    position = lax.axis_index("sub")
    slots = jnp.arange(sub_count, dtype=jnp.int32)
    earlier_mask = (slots < position)[:, None, None, None]
    later_mask = (slots > position)[:, None, None, None]
    zero_value = jnp.float32(0.0)
    inner_kv = jnp.sum(jnp.where(earlier_mask, every_kv, zero_value), axis=0)
    inner_grad = jnp.sum(jnp.where(later_mask, every_grad, zero_value), axis=0)
    share_rows = kv_local.shape[1] // sub_count
    start_row = position * share_rows
    share_kv = lax.dynamic_slice_in_dim(jnp.sum(every_kv, axis=0), start_row, share_rows, 1)
    share_grad = lax.dynamic_slice_in_dim(jnp.sum(every_grad, axis=0), start_row, share_rows, 1)
    share_zero = jnp.zeros_like(share_kv)
    outer_kv = carried_in(share_kv, "ctx", add_one, share_zero, False)
    outer_grad = carried_in(share_grad, "ctx", add_one, share_zero, True)
    full_kv, full_grad = (
        lax.all_gather(outer_kv, "sub", axis=1, tiled=True),
        lax.all_gather(outer_grad, "sub", axis=1, tiled=True),
    )
    before = (full_kv + inner_kv).astype(jnp.bfloat16)
    after = (full_grad + inner_grad).astype(jnp.bfloat16)
    row_index = jnp.arange(row_count, dtype=jnp.int32)
    causal = row_index[:, None] >= row_index[None, :]
    reg_mask = reg_offset[:, None] >= row_index[None, :]
    zero = jnp.float32(0.0)
    out_scores = jnp.where(
        causal,
        jnp.einsum("the,she->hts", grad_heads, value_heads, preferred_element_type=jnp.float32),
        zero,
    ).astype(jnp.bfloat16)
    qk_scores = jnp.where(
        causal,
        jnp.einsum("thd,shd->hts", query_heads, key_heads, preferred_element_type=jnp.float32),
        zero,
    ).astype(jnp.bfloat16)
    reg_out_scores = jnp.where(
        reg_mask,
        jnp.einsum("jhe,she->hjs", regg_heads, value_heads, preferred_element_type=jnp.float32),
        zero,
    ).astype(jnp.bfloat16)
    reg_qk_scores = jnp.where(
        reg_mask,
        jnp.einsum("jhd,shd->hjs", regq_heads, key_heads, preferred_element_type=jnp.float32),
        zero,
    ).astype(jnp.bfloat16)
    grad_q = jnp.einsum(
        "hts,shd->thd", out_scores, key_heads, preferred_element_type=jnp.float32
    ) + jnp.einsum("the,hde->thd", grad_heads, before, preferred_element_type=jnp.float32)
    grad_rq = jnp.einsum(
        "hjs,shd->jhd", reg_out_scores, key_heads, preferred_element_type=jnp.float32
    ) + jnp.einsum("jhe,hde->jhd", regg_heads, before, preferred_element_type=jnp.float32)
    grad_k = (
        jnp.einsum("hts,thd->shd", out_scores, query_heads, preferred_element_type=jnp.float32)
        + jnp.einsum("hjs,jhd->shd", reg_out_scores, regq_heads, preferred_element_type=jnp.float32)
        + jnp.einsum("she,hde->shd", value_heads, after, preferred_element_type=jnp.float32)
    )
    grad_v = (
        jnp.einsum("hts,the->she", qk_scores, grad_heads, preferred_element_type=jnp.float32)
        + jnp.einsum("hjs,jhe->she", reg_qk_scores, regg_heads, preferred_element_type=jnp.float32)
        + jnp.einsum("shd,hde->she", key_heads, after, preferred_element_type=jnp.float32)
    )
    width = HEADS * HEAD
    return (
        (grad_q * factor).astype(jnp.bfloat16).reshape(row_count, width),
        (grad_k * factor).astype(jnp.bfloat16).reshape(row_count, width),
        (grad_v * factor).astype(jnp.bfloat16).reshape(row_count, width),
        (grad_rq * factor).astype(jnp.bfloat16).reshape(reg_count, width),
    )


def contract(lhs, rhs, lhs_dim, rhs_dim):
    return lax.dot_general(
        lhs, rhs, (((lhs_dim,), (rhs_dim,)), ((), ())), preferred_element_type=jnp.float32
    )


def kernel(
    factor,
    q_hbm, k_hbm, v_hbm, g_hbm, rq_hbm, rg_hbm, off_ref,
    out_q, out_k, out_v, out_rq,
    qa, ga, ka, va, mine, pair, cross_out, cross_in, chain_in, chain_out, other, full, full16,
    acc_q, acc_k, acc_v,
    load_sem, pair_send, pair_recv, cross_send, cross_recv, chain_send, chain_recv,
    own_send, other_send, relay_send, full_recv,
):
    ctx_count, sub_count = lax.axis_size("ctx"), lax.axis_size("sub")
    each = HEADS // sub_count
    units = each * PARTS
    z, s = lax.axis_index("ctx"), lax.axis_index("sub")
    a, c = s // 2, s % 2
    partner = {"sub": 2 * a + 1 - c}
    across = {"sub": 2 * (1 - a) + c}
    rows, regs = ka.shape[0], rq_hbm.shape[0]

    loads = [
        pltpu.make_async_copy(k_hbm, ka, load_sem.at[0]),
        pltpu.make_async_copy(v_hbm, va, load_sem.at[1]),
        pltpu.make_async_copy(q_hbm, qa.at[pl.ds(0, rows)], load_sem.at[2]),
        pltpu.make_async_copy(g_hbm, ga.at[pl.ds(0, rows)], load_sem.at[3]),
        pltpu.make_async_copy(rq_hbm, qa.at[pl.ds(rows, regs)], load_sem.at[4]),
        pltpu.make_async_copy(rg_hbm, ga.at[pl.ds(rows, regs)], load_sem.at[5]),
    ]
    for load in loads:
        load.start()

    barrier = pltpu.get_barrier_semaphore()
    has_prev, has_next = z > 0, z < ctx_count - 1
    for target in (partner, across):
        pl.semaphore_signal(barrier, inc=1, device_id=target, device_id_type=MESH)

    @pl.when(has_prev)
    def _():
        pl.semaphore_signal(barrier, inc=1, device_id={"ctx": z - 1}, device_id_type=MESH)

    @pl.when(has_next)
    def _():
        pl.semaphore_signal(barrier, inc=1, device_id={"ctx": z + 1}, device_id_type=MESH)

    def cols(h):
        return pl.ds(pl.multiple_of(h * HEAD, HEAD), HEAD)

    def whole(h):
        return pl.ds(h * PARTS, PARTS)

    def remote(src, dst, send, recv, target):
        return pltpu.make_async_remote_copy(
            src_ref=src, dst_ref=dst, send_sem=send, recv_sem=recv,
            device_id=target, device_id_type=MESH,
        )

    def pair_copy(k, h):
        return remote(mine.at[k, whole(h)], pair.at[k, whole(h)], pair_send.at[k, h], pair_recv.at[k, h], partner)

    def cross_copy(k, i):
        return remote(
            cross_out.at[k, i], cross_in.at[k, i], cross_send.at[k, i], cross_recv.at[k, i], across
        )

    def chain_copy(k, i, target):
        return remote(
            chain_out.at[k, i], chain_in.at[k, i], chain_send.at[k, i], chain_recv.at[k, i],
            {"ctx": target},
        )

    def own_copy(k, i):
        h = s * units + i
        return remote(full.at[k, h], full.at[k, h], own_send.at[k, i], full_recv.at[k, h], partner)

    def other_copy(k, i):
        return remote(
            other.at[k, i], full.at[k, s * units + i], other_send.at[k, i],
            full_recv.at[k, s * units + i], across,
        )

    def relay_copy(k, i):
        h = across["sub"] * units + i
        return remote(full.at[k, h], full.at[k, h], relay_send.at[k, i], full_recv.at[k, h], partner)

    first = jnp.where(2 * z >= ctx_count, 1, 0)
    kinds = (first, 1 - first)

    def state(h):
        piece = (PARTS, HEAD // PARTS, HEAD)
        mine[0, whole(h)] = contract(ka[:, cols(h)], va[:, cols(h)], 0, 0).reshape(piece)
        mine[1, whole(h)] = contract(qa[:, cols(h)], ga[:, cols(h)], 0, 0).reshape(piece)

    for load in loads:
        load.wait()
    greeted = 2 + jnp.where(has_prev, 1, 0) + jnp.where(has_next, 1, 0)

    for i in range(each):
        state((2 * (1 - a) + 1 - c) * each + i)
    pl.semaphore_wait(barrier, greeted)
    for i in range(each):
        for k in kinds:
            pair_copy(k, (2 * (1 - a) + 1 - c) * each + i).start()
    for i in range(each):
        state(across["sub"] * each + i)
    for k in kinds:
        for i in range(each):
            h = across["sub"] * each + i
            pair_copy(k, h).wait_recv()
            cross_out[k, whole(i)] = mine[k, whole(h)] + pair[k, whole(h)]
            for part in range(PARTS):
                cross_copy(k, i * PARTS + part).start()
    for i in range(each):
        state((2 * a + 1 - c) * each + i)
    for i in range(each):
        for k in kinds:
            pair_copy(k, (2 * a + 1 - c) * each + i).start()
    for i in range(each):
        state(s * each + i)
    for side in range(2):
        for i in range(each):
            pair_copy(c, (2 * side + c) * each + i).start()

    place = lax.broadcasted_iota(jnp.int32, (rows, rows), 0)
    time = lax.broadcasted_iota(jnp.int32, (rows, rows), 1)
    reg_place = lax.broadcasted_iota(jnp.int32, (rows, regs), 0)

    def masked(scores):
        zero = jnp.float32(0.0)
        regular = jnp.where(time >= place, scores[:, :rows], zero)
        register = jnp.where(off_ref[...] >= reg_place, scores[:, rows:], zero)
        return jnp.concatenate([regular, register], axis=1).astype(jnp.bfloat16)

    def scores(h):
        at = cols(h)
        key, value, query, grad = ka[:, at], va[:, at], qa[:, at], ga[:, at]
        out_scores = masked(contract(value, grad, 1, 1))
        qk_scores = masked(contract(key, query, 1, 1))
        acc_q[:, at] = contract(out_scores, key, 0, 0)
        acc_k[:, at] = contract(out_scores, query, 1, 0)
        acc_v[:, at] = contract(qk_scores, grad, 1, 0)

    def some_scores(low, high):
        lax.fori_loop(low, high, lambda h, _: (scores(h), 0)[1], 0)

    def chain(k):
        has_in = jnp.where(k == 0, has_prev, has_next)
        has_out = jnp.where(k == 0, has_next, has_prev)
        target = jnp.where(k == 0, z + 1, z - 1)
        ahead = a == k
        for i in range(each):
            pair_copy(k, s * each + i).wait_recv()
        for i in range(units):
            h = s * units + i
            cross_copy(k, i).wait_recv()

            @pl.when(has_in)
            def _():
                chain_copy(k, i, target).wait_recv()

            @pl.when(jnp.logical_not(has_in))
            def _():
                chain_in[k, i] = jnp.zeros((HEAD // PARTS, HEAD), jnp.float32)

            @pl.when(has_out)
            def _():
                chain_out[k, i] = (chain_in[k, i] + (mine[k, h] + pair[k, h])) + cross_in[k, i]
                chain_copy(k, i, target).start()

            carried = chain_in[k, i]
            zero = jnp.float32(0.0)
            own = mine[k, h] + pair[k, h]
            other[k, i] = carried + jnp.where(ahead, own, zero)
            other_copy(k, i).start()
            full[k, h] = carried + jnp.where(ahead, zero, cross_in[k, i])
            own_copy(k, i).start()

    def relay(k):
        for i in range(units):
            h = across["sub"] * units + i
            remote(
                other.at[k, i], full.at[k, h], other_send.at[k, i], full_recv.at[k, h], across
            ).wait_recv()
            relay_copy(k, i).start()

    def full_wait(h):
        for k in range(2):
            for part in range(PARTS):
                u = h * PARTS + part
                remote(
                    full.at[k, u], full.at[k, u], own_send.at[0, 0], full_recv.at[k, u], partner
                ).wait_recv()

    def finish(h):
        at = cols(h)
        square = (HEAD, HEAD)
        joined = full[1 - c, whole(h)] + pair[1 - c, whole(h)]
        full16[1 - c, h] = joined.reshape(square).astype(jnp.bfloat16)
        full16[c, h] = full[c, whole(h)].reshape(square).astype(jnp.bfloat16)
        before, after = full16[0, h], full16[1, h]
        sums = (acc_q[:, at] + contract(ga[:, at], before, 1, 1)) * factor
        out_q[:, at] = sums[:rows].astype(jnp.bfloat16)
        out_rq[:, at] = sums[rows:].astype(jnp.bfloat16)
        out_k[:, at] = ((acc_k[:, at] + contract(va[:, at], after, 1, 1)) * factor).astype(jnp.bfloat16)
        out_v[:, at] = ((acc_v[:, at] + contract(ka[:, at], after, 1, 0)) * factor).astype(jnp.bfloat16)

    some_scores(0, 3)
    chain(kinds[0])
    some_scores(3, 5)
    chain(kinds[1])
    relay(kinds[0])
    some_scores(5, HEADS)
    for side in range(2):
        for i in range(each):
            pair_copy(1 - c, (2 * side + 1 - c) * each + i).wait_recv()
    for i in range(each):
        finish(s * each + i)
    for i in range(each):
        h = (2 * a + 1 - c) * each + i
        full_wait(h)
        finish(h)
    relay(kinds[1])
    for i in range(each):
        finish(across["sub"] * each + i)
    for i in range(each):
        h = (2 * (1 - a) + 1 - c) * each + i
        full_wait(h)
        finish(h)

    for k in range(2):
        for i in range(each):
            for side in range(2):
                pair_copy(k, (2 * side + 1 - c) * each + i).wait_send()
        for i in range(units):
            cross_copy(k, i).wait_send()
            other_copy(k, i).wait_send()
            own_copy(k, i).wait_send()
            relay_copy(k, i).wait_send()

            @pl.when((has_next, has_prev)[k])
            def _():
                chain_copy(k, i, (z + 1, z - 1)[k]).wait_send()
    for side in range(2):
        for i in range(each):
            pair_copy(c, (2 * side + c) * each + i).wait_send()


def store_all(*refs):
    sources, results, held, in_sem, out_sem = refs[:4], refs[4:8], refs[8:12], refs[12], refs[13]
    loads = [pltpu.make_async_copy(sources[i], held[i], in_sem.at[i]) for i in range(4)]
    stores = [pltpu.make_async_copy(held[i], results[i], out_sem.at[i]) for i in range(4)]
    for load in loads:
        load.start()
    for load, store in zip(loads, stores):
        load.wait()
        store.start()
    for store in stores:
        store.wait()


def fused(query_rows, key_rows, value_rows, out_grad, reg_query, reg_out_grad, reg_offset):
    rows, width = query_rows.shape
    regs = reg_query.shape[0]
    sub_count = lax.axis_size("sub")
    factor = 1.0 / math.sqrt(HEAD * rows * lax.axis_size("ctx") * sub_count)
    each = HEADS // sub_count
    all_states = pltpu.VMEM((2, HEADS * PARTS, HEAD // PARTS, HEAD), jnp.float32)
    few_states = pltpu.VMEM((2, each * PARTS, HEAD // PARTS, HEAD), jnp.float32)
    all_sems = pltpu.SemaphoreType.DMA((2, HEADS))
    unit_sems = pltpu.SemaphoreType.DMA((2, HEADS * PARTS))
    few_sems = pltpu.SemaphoreType.DMA((2, each * PARTS))
    vmem = pl.BlockSpec(memory_space=pltpu.VMEM)
    hbm = pl.BlockSpec(memory_space=pltpu.HBM)
    shapes = (
        jax.ShapeDtypeStruct((rows, width), jnp.bfloat16),
        jax.ShapeDtypeStruct((rows, width), jnp.bfloat16),
        jax.ShapeDtypeStruct((rows, width), jnp.bfloat16),
        jax.ShapeDtypeStruct((regs, width), jnp.bfloat16),
    )
    results = pl.pallas_call(
        functools.partial(kernel, factor),
        out_shape=shapes,
        in_specs=[hbm] * 6 + [vmem],
        out_specs=(vmem,) * 4,
        scratch_shapes=[
            pltpu.VMEM((rows + regs, width), jnp.bfloat16),
            pltpu.VMEM((rows + regs, width), jnp.bfloat16),
            pltpu.VMEM((rows, width), jnp.bfloat16),
            pltpu.VMEM((rows, width), jnp.bfloat16),
            all_states, all_states,
            few_states, few_states, few_states, few_states, few_states,
            all_states,
            pltpu.VMEM((2, HEADS, HEAD, HEAD), jnp.bfloat16),
            pltpu.VMEM((rows + regs, width), jnp.float32),
            pltpu.VMEM((rows, width), jnp.float32),
            pltpu.VMEM((rows, width), jnp.float32),
            pltpu.SemaphoreType.DMA((6,)),
            all_sems, all_sems,
            few_sems, few_sems, few_sems, few_sems,
            few_sems, few_sems, few_sems, unit_sems,
        ],
        compiler_params=pltpu.CompilerParams(
            collective_id=0, has_side_effects=True, vmem_limit_bytes=63400 * 1024
        ),
    )(
        query_rows, key_rows, value_rows, out_grad, reg_query, reg_out_grad,
        reg_offset.reshape(1, regs),
    )
    return pl.pallas_call(
        store_all,
        out_shape=shapes,
        in_specs=[hbm] * 4,
        out_specs=(hbm,) * 4,
        scratch_shapes=[pltpu.VMEM(shape.shape, shape.dtype) for shape in shapes]
        + [pltpu.SemaphoreType.DMA((4,)), pltpu.SemaphoreType.DMA((4,))],
        compiler_params=pltpu.CompilerParams(vmem_limit_bytes=63400 * 1024),
    )(*results)


def solution(mesh):
    placed = (
        P(("grp", "ctx", "sub"), None),
        P(("grp", "ctx", "sub"), None),
        P(("grp", "ctx", "sub"), None),
        P(("grp", "ctx", "sub"), None),
        P(("grp", "ctx", "sub"), None),
        P(("grp", "ctx", "sub"), None),
        P(("grp", "ctx", "sub")),
    )
    return jax.shard_map(
        fused if mesh.shape["sub"] == 4 else local,
        mesh=mesh,
        in_specs=placed,
        out_specs=(
            P(("grp", "ctx", "sub"), None),
            P(("grp", "ctx", "sub"), None),
            P(("grp", "ctx", "sub"), None),
            P(("grp", "ctx", "sub"), None),
        ),
        check_vma=False,
    )
```

```python
import functools
import math

import jax
import jax.numpy as jnp
from jax import lax
from jax.experimental import pallas as pl
from jax.experimental.pallas import tpu as pltpu
from jax.sharding import PartitionSpec as P

HEADS = 8
HEAD = 128
MESH = pl.DeviceIdType.MESH
PARTS = 2


def carried_in(value, axis, join, neutral, backward):
    count, mine = (lax.axis_size(axis), lax.axis_index(axis))
    pieces = lax.all_gather(value, axis)
    if backward:
        pieces = pieces[::-1]
        mine = count - 1 - mine
    running = jnp.full_like(value, 0) + jnp.asarray(neutral, value.dtype)

    def hop(position, running):
        longer = join(running, pieces[position])
        return jnp.where(position < mine, longer, running)

    return lax.fori_loop(0, count - 1, hop, running)


def add_one(earlier, later):
    return earlier + later


def local(query_rows, key_rows, value_rows, out_grad, reg_query, reg_out_grad, reg_offset):
    row_count = query_rows.shape[0]
    reg_count = reg_query.shape[0]
    total_rows = row_count * lax.axis_size("ctx") * lax.axis_size("sub")
    factor = 1.0 / math.sqrt(HEAD * total_rows)
    query_heads = query_rows.reshape(row_count, HEADS, HEAD)
    key_heads = key_rows.reshape(row_count, HEADS, HEAD)
    value_heads = value_rows.reshape(row_count, HEADS, HEAD)
    grad_heads = out_grad.reshape(row_count, HEADS, HEAD)
    regq_heads = reg_query.reshape(reg_count, HEADS, HEAD)
    regg_heads = reg_out_grad.reshape(reg_count, HEADS, HEAD)
    kv_local = jnp.einsum(
        "shd,she->hde", key_heads, value_heads, preferred_element_type=jnp.float32
    )
    grad_local = jnp.einsum(
        "thd,the->hde", query_heads, grad_heads, preferred_element_type=jnp.float32
    ) + jnp.einsum("jhd,jhe->hde", regq_heads, regg_heads, preferred_element_type=jnp.float32)
    every_kv, every_grad = (
        lax.all_gather(kv_local[None], "sub", axis=0, tiled=True),
        lax.all_gather(grad_local[None], "sub", axis=0, tiled=True),
    )
    sub_count = lax.axis_size("sub")
    position = lax.axis_index("sub")
    slots = jnp.arange(sub_count, dtype=jnp.int32)
    earlier_mask = (slots < position)[:, None, None, None]
    later_mask = (slots > position)[:, None, None, None]
    zero_value = jnp.float32(0.0)
    inner_kv = jnp.sum(jnp.where(earlier_mask, every_kv, zero_value), axis=0)
    inner_grad = jnp.sum(jnp.where(later_mask, every_grad, zero_value), axis=0)
    share_rows = kv_local.shape[1] // sub_count
    start_row = position * share_rows
    share_kv = lax.dynamic_slice_in_dim(jnp.sum(every_kv, axis=0), start_row, share_rows, 1)
    share_grad = lax.dynamic_slice_in_dim(jnp.sum(every_grad, axis=0), start_row, share_rows, 1)
    share_zero = jnp.zeros_like(share_kv)
    outer_kv = carried_in(share_kv, "ctx", add_one, share_zero, False)
    outer_grad = carried_in(share_grad, "ctx", add_one, share_zero, True)
    full_kv, full_grad = (
        lax.all_gather(outer_kv, "sub", axis=1, tiled=True),
        lax.all_gather(outer_grad, "sub", axis=1, tiled=True),
    )
    before = (full_kv + inner_kv).astype(jnp.bfloat16)
    after = (full_grad + inner_grad).astype(jnp.bfloat16)
    row_index = jnp.arange(row_count, dtype=jnp.int32)
    causal = row_index[:, None] >= row_index[None, :]
    reg_mask = reg_offset[:, None] >= row_index[None, :]
    zero = jnp.float32(0.0)
    out_scores = jnp.where(
        causal,
        jnp.einsum("the,she->hts", grad_heads, value_heads, preferred_element_type=jnp.float32),
        zero,
    ).astype(jnp.bfloat16)
    qk_scores = jnp.where(
        causal,
        jnp.einsum("thd,shd->hts", query_heads, key_heads, preferred_element_type=jnp.float32),
        zero,
    ).astype(jnp.bfloat16)
    reg_out_scores = jnp.where(
        reg_mask,
        jnp.einsum("jhe,she->hjs", regg_heads, value_heads, preferred_element_type=jnp.float32),
        zero,
    ).astype(jnp.bfloat16)
    reg_qk_scores = jnp.where(
        reg_mask,
        jnp.einsum("jhd,shd->hjs", regq_heads, key_heads, preferred_element_type=jnp.float32),
        zero,
    ).astype(jnp.bfloat16)
    grad_q = jnp.einsum(
        "hts,shd->thd", out_scores, key_heads, preferred_element_type=jnp.float32
    ) + jnp.einsum("the,hde->thd", grad_heads, before, preferred_element_type=jnp.float32)
    grad_rq = jnp.einsum(
        "hjs,shd->jhd", reg_out_scores, key_heads, preferred_element_type=jnp.float32
    ) + jnp.einsum("jhe,hde->jhd", regg_heads, before, preferred_element_type=jnp.float32)
    grad_k = (
        jnp.einsum("hts,thd->shd", out_scores, query_heads, preferred_element_type=jnp.float32)
        + jnp.einsum("hjs,jhd->shd", reg_out_scores, regq_heads, preferred_element_type=jnp.float32)
        + jnp.einsum("she,hde->shd", value_heads, after, preferred_element_type=jnp.float32)
    )
    grad_v = (
        jnp.einsum("hts,the->she", qk_scores, grad_heads, preferred_element_type=jnp.float32)
        + jnp.einsum("hjs,jhe->she", reg_qk_scores, regg_heads, preferred_element_type=jnp.float32)
        + jnp.einsum("shd,hde->she", key_heads, after, preferred_element_type=jnp.float32)
    )
    width = HEADS * HEAD
    return (
        (grad_q * factor).astype(jnp.bfloat16).reshape(row_count, width),
        (grad_k * factor).astype(jnp.bfloat16).reshape(row_count, width),
        (grad_v * factor).astype(jnp.bfloat16).reshape(row_count, width),
        (grad_rq * factor).astype(jnp.bfloat16).reshape(reg_count, width),
    )


def contract(lhs, rhs, lhs_dim, rhs_dim):
    return lax.dot_general(
        lhs, rhs, (((lhs_dim,), (rhs_dim,)), ((), ())), preferred_element_type=jnp.float32
    )


def kernel(
    factor,
    q_hbm, k_hbm, v_hbm, g_hbm, rq_hbm, rg_hbm, off_hbm,
    out_q, out_k, out_v, out_rq,
    off_ref, qa, ga, ka, va, mine, pair, cross_out, cross_in, chain_in, chain_out, other, full, full16,
    acc_q, acc_k, acc_v,
    load_sem, pair_send, pair_recv, cross_send, cross_recv, chain_send, chain_recv,
    own_send, other_send, relay_send, full_recv,
):
    ctx_count, sub_count = lax.axis_size("ctx"), lax.axis_size("sub")
    each = HEADS // sub_count
    units = each * PARTS
    z, s = lax.axis_index("ctx"), lax.axis_index("sub")
    a, c = s // 2, s % 2
    partner = {"sub": 2 * a + 1 - c}
    across = {"sub": 2 * (1 - a) + c}
    rows, regs = ka.shape[0], rq_hbm.shape[0]

    loads = [
        pltpu.make_async_copy(k_hbm, ka, load_sem.at[0]),
        pltpu.make_async_copy(v_hbm, va, load_sem.at[1]),
        pltpu.make_async_copy(q_hbm, qa.at[pl.ds(0, rows)], load_sem.at[2]),
        pltpu.make_async_copy(g_hbm, ga.at[pl.ds(0, rows)], load_sem.at[3]),
        pltpu.make_async_copy(rq_hbm, qa.at[pl.ds(rows, regs)], load_sem.at[4]),
        pltpu.make_async_copy(rg_hbm, ga.at[pl.ds(rows, regs)], load_sem.at[5]),
    ]
    load_offset = pltpu.make_async_copy(off_hbm, off_ref, load_sem.at[6])
    for load in loads:
        load.start()
    load_offset.start()

    barrier = pltpu.get_barrier_semaphore()
    has_prev, has_next = z > 0, z < ctx_count - 1
    for target in (partner, across):
        pl.semaphore_signal(barrier, inc=1, device_id=target, device_id_type=MESH)

    @pl.when(has_prev)
    def _():
        pl.semaphore_signal(barrier, inc=1, device_id={"ctx": z - 1}, device_id_type=MESH)

    @pl.when(has_next)
    def _():
        pl.semaphore_signal(barrier, inc=1, device_id={"ctx": z + 1}, device_id_type=MESH)

    def cols(h):
        return pl.ds(pl.multiple_of(h * HEAD, HEAD), HEAD)

    def whole(h):
        return pl.ds(h * PARTS, PARTS)

    def remote(src, dst, send, recv, target):
        return pltpu.make_async_remote_copy(
            src_ref=src, dst_ref=dst, send_sem=send, recv_sem=recv,
            device_id=target, device_id_type=MESH,
        )

    def pair_copy(k, h):
        return remote(mine.at[k, whole(h)], pair.at[k, whole(h)], pair_send.at[k, h], pair_recv.at[k, h], partner)

    def cross_copy(k, i):
        return remote(
            cross_out.at[k, i], cross_in.at[k, i], cross_send.at[k, i], cross_recv.at[k, i], across
        )

    def chain_copy(k, i, target):
        return remote(
            chain_out.at[k, i], chain_in.at[k, i], chain_send.at[k, i], chain_recv.at[k, i],
            {"ctx": target},
        )

    def own_copy(k, i):
        h = s * units + i
        return remote(full.at[k, h], full.at[k, h], own_send.at[k, i], full_recv.at[k, h], partner)

    def other_copy(k, i):
        return remote(
            other.at[k, i], full.at[k, s * units + i], other_send.at[k, i],
            full_recv.at[k, s * units + i], across,
        )

    def relay_copy(k, i):
        h = across["sub"] * units + i
        return remote(full.at[k, h], full.at[k, h], relay_send.at[k, i], full_recv.at[k, h], partner)

    first = jnp.where(2 * z >= ctx_count, 1, 0)
    kinds = (first, 1 - first)

    def state(h):
        piece = (PARTS, HEAD // PARTS, HEAD)
        mine[0, whole(h)] = contract(ka[:, cols(h)], va[:, cols(h)], 0, 0).reshape(piece)
        mine[1, whole(h)] = contract(qa[:, cols(h)], ga[:, cols(h)], 0, 0).reshape(piece)

    for load in loads:
        load.wait()
    greeted = 2 + jnp.where(has_prev, 1, 0) + jnp.where(has_next, 1, 0)

    for i in range(each):
        state((2 * (1 - a) + 1 - c) * each + i)
    pl.semaphore_wait(barrier, greeted)
    for i in range(each):
        for k in kinds:
            pair_copy(k, (2 * (1 - a) + 1 - c) * each + i).start()
    for i in range(each):
        state(across["sub"] * each + i)
    for k in kinds:
        for i in range(each):
            h = across["sub"] * each + i
            pair_copy(k, h).wait_recv()
            cross_out[k, whole(i)] = mine[k, whole(h)] + pair[k, whole(h)]
            for part in range(PARTS):
                cross_copy(k, i * PARTS + part).start()
    for i in range(each):
        state((2 * a + 1 - c) * each + i)
    for i in range(each):
        for k in kinds:
            pair_copy(k, (2 * a + 1 - c) * each + i).start()
    for i in range(each):
        state(s * each + i)
    for side in range(2):
        for i in range(each):
            pair_copy(c, (2 * side + c) * each + i).start()

    place = lax.broadcasted_iota(jnp.int32, (rows, rows), 0)
    time = lax.broadcasted_iota(jnp.int32, (rows, rows), 1)
    reg_place = lax.broadcasted_iota(jnp.int32, (rows, regs), 0)

    def masked(scores):
        zero = jnp.float32(0.0)
        regular = jnp.where(time >= place, scores[:, :rows], zero)
        register = jnp.where(off_ref[...] >= reg_place, scores[:, rows:], zero)
        return jnp.concatenate([regular, register], axis=1).astype(jnp.bfloat16)

    def scores(h):
        at = cols(h)
        key, value, query, grad = ka[:, at], va[:, at], qa[:, at], ga[:, at]
        out_scores = masked(contract(value, grad, 1, 1))
        qk_scores = masked(contract(key, query, 1, 1))
        acc_q[:, at] = contract(out_scores, key, 0, 0)
        acc_k[:, at] = contract(out_scores, query, 1, 0)
        acc_v[:, at] = contract(qk_scores, grad, 1, 0)

    def some_scores(low, high):
        lax.fori_loop(low, high, lambda h, _: (scores(h), 0)[1], 0)

    def chain(k):
        has_in = jnp.where(k == 0, has_prev, has_next)
        has_out = jnp.where(k == 0, has_next, has_prev)
        target = jnp.where(k == 0, z + 1, z - 1)
        ahead = a == k
        for i in range(each):
            pair_copy(k, s * each + i).wait_recv()
        for i in range(units):
            h = s * units + i
            cross_copy(k, i).wait_recv()

            @pl.when(has_in)
            def _():
                chain_copy(k, i, target).wait_recv()

            @pl.when(jnp.logical_not(has_in))
            def _():
                chain_in[k, i] = jnp.zeros((HEAD // PARTS, HEAD), jnp.float32)

            @pl.when(has_out)
            def _():
                chain_out[k, i] = (chain_in[k, i] + (mine[k, h] + pair[k, h])) + cross_in[k, i]
                chain_copy(k, i, target).start()

            carried = chain_in[k, i]
            zero = jnp.float32(0.0)
            own = mine[k, h] + pair[k, h]
            other[k, i] = carried + jnp.where(ahead, own, zero)
            other_copy(k, i).start()
            full[k, h] = carried + jnp.where(ahead, zero, cross_in[k, i])
            own_copy(k, i).start()

    def relay(k):
        for i in range(units):
            h = across["sub"] * units + i
            remote(
                other.at[k, i], full.at[k, h], other_send.at[k, i], full_recv.at[k, h], across
            ).wait_recv()
            relay_copy(k, i).start()

    def full_wait(h):
        for k in range(2):
            for part in range(PARTS):
                u = h * PARTS + part
                remote(
                    full.at[k, u], full.at[k, u], own_send.at[0, 0], full_recv.at[k, u], partner
                ).wait_recv()

    def finish(h):
        at = cols(h)
        square = (HEAD, HEAD)
        joined = full[1 - c, whole(h)] + pair[1 - c, whole(h)]
        full16[1 - c, h] = joined.reshape(square).astype(jnp.bfloat16)
        full16[c, h] = full[c, whole(h)].reshape(square).astype(jnp.bfloat16)
        before, after = full16[0, h], full16[1, h]
        sums = (acc_q[:, at] + contract(ga[:, at], before, 1, 1)) * factor
        out_q[:, at] = sums[:rows].astype(jnp.bfloat16)
        out_rq[:, at] = sums[rows:].astype(jnp.bfloat16)
        out_k[:, at] = ((acc_k[:, at] + contract(va[:, at], after, 1, 1)) * factor).astype(jnp.bfloat16)
        out_v[:, at] = ((acc_v[:, at] + contract(ka[:, at], after, 1, 0)) * factor).astype(jnp.bfloat16)

    load_offset.wait()
    some_scores(0, 3)
    chain(kinds[0])
    some_scores(3, 5)
    chain(kinds[1])
    relay(kinds[0])
    some_scores(5, HEADS)
    for side in range(2):
        for i in range(each):
            pair_copy(1 - c, (2 * side + 1 - c) * each + i).wait_recv()
    for i in range(each):
        finish(s * each + i)
    for i in range(each):
        h = (2 * a + 1 - c) * each + i
        full_wait(h)
        finish(h)
    relay(kinds[1])
    for i in range(each):
        finish(across["sub"] * each + i)
    for i in range(each):
        h = (2 * (1 - a) + 1 - c) * each + i
        full_wait(h)
        finish(h)

    for k in range(2):
        for i in range(each):
            for side in range(2):
                pair_copy(k, (2 * side + 1 - c) * each + i).wait_send()
        for i in range(units):
            cross_copy(k, i).wait_send()
            other_copy(k, i).wait_send()
            own_copy(k, i).wait_send()
            relay_copy(k, i).wait_send()

            @pl.when((has_next, has_prev)[k])
            def _():
                chain_copy(k, i, (z + 1, z - 1)[k]).wait_send()
    for side in range(2):
        for i in range(each):
            pair_copy(c, (2 * side + c) * each + i).wait_send()


def store_all(*refs):
    copies = [pltpu.make_async_copy(refs[i], refs[4 + i], refs[8].at[i]) for i in range(4)]
    for copy in copies:
        copy.start()
    for copy in copies:
        copy.wait()


def fused(query_rows, key_rows, value_rows, out_grad, reg_query, reg_out_grad, reg_offset):
    rows, width = query_rows.shape
    regs = reg_query.shape[0]
    sub_count = lax.axis_size("sub")
    factor = 1.0 / math.sqrt(HEAD * rows * lax.axis_size("ctx") * sub_count)
    each = HEADS // sub_count
    all_states = pltpu.VMEM((2, HEADS * PARTS, HEAD // PARTS, HEAD), jnp.float32)
    few_states = pltpu.VMEM((2, each * PARTS, HEAD // PARTS, HEAD), jnp.float32)
    all_sems = pltpu.SemaphoreType.DMA((2, HEADS))
    unit_sems = pltpu.SemaphoreType.DMA((2, HEADS * PARTS))
    few_sems = pltpu.SemaphoreType.DMA((2, each * PARTS))
    vmem = pl.BlockSpec(memory_space=pltpu.VMEM)
    hbm = pl.BlockSpec(memory_space=pltpu.HBM)
    shapes = (
        jax.ShapeDtypeStruct((rows, width), jnp.bfloat16),
        jax.ShapeDtypeStruct((rows, width), jnp.bfloat16),
        jax.ShapeDtypeStruct((rows, width), jnp.bfloat16),
        jax.ShapeDtypeStruct((regs, width), jnp.bfloat16),
    )
    results = pl.pallas_call(
        functools.partial(kernel, factor),
        out_shape=shapes,
        in_specs=[hbm] * 7,
        out_specs=(vmem,) * 4,
        scratch_shapes=[
            pltpu.VMEM((1, regs), jnp.int32),
            pltpu.VMEM((rows + regs, width), jnp.bfloat16),
            pltpu.VMEM((rows + regs, width), jnp.bfloat16),
            pltpu.VMEM((rows, width), jnp.bfloat16),
            pltpu.VMEM((rows, width), jnp.bfloat16),
            all_states, all_states,
            few_states, few_states, few_states, few_states, few_states,
            all_states,
            pltpu.VMEM((2, HEADS, HEAD, HEAD), jnp.bfloat16),
            pltpu.VMEM((rows + regs, width), jnp.float32),
            pltpu.VMEM((rows, width), jnp.float32),
            pltpu.VMEM((rows, width), jnp.float32),
            pltpu.SemaphoreType.DMA((7,)),
            all_sems, all_sems,
            few_sems, few_sems, few_sems, few_sems,
            few_sems, few_sems, few_sems, unit_sems,
        ],
        compiler_params=pltpu.CompilerParams(
            collective_id=0, has_side_effects=True, vmem_limit_bytes=40960 * 1024
        ),
    )(
        *[
            pltpu.with_memory_space_constraint(array, pltpu.HBM)
            for array in (query_rows, key_rows, value_rows, out_grad, reg_query, reg_out_grad)
        ],
        pltpu.with_memory_space_constraint(reg_offset.reshape(1, regs), pltpu.HBM),
    )
    return pl.pallas_call(
        store_all,
        out_shape=shapes,
        in_specs=[vmem] * 4,
        out_specs=(hbm,) * 4,
        scratch_shapes=[pltpu.SemaphoreType.DMA((4,))],
        compiler_params=pltpu.CompilerParams(vmem_limit_bytes=1024 * 1024),
    )(*results)


def solution(mesh):
    placed = (
        P(("grp", "ctx", "sub"), None),
        P(("grp", "ctx", "sub"), None),
        P(("grp", "ctx", "sub"), None),
        P(("grp", "ctx", "sub"), None),
        P(("grp", "ctx", "sub"), None),
        P(("grp", "ctx", "sub"), None),
        P(("grp", "ctx", "sub")),
    )
    return jax.shard_map(
        fused if mesh.shape["sub"] == 4 else local,
        mesh=mesh,
        in_specs=placed,
        out_specs=(
            P(("grp", "ctx", "sub"), None),
            P(("grp", "ctx", "sub"), None),
            P(("grp", "ctx", "sub"), None),
            P(("grp", "ctx", "sub"), None),
        ),
        check_vma=False,
    )
```

```python
import functools
import math

import jax
import jax.numpy as jnp
from jax import lax
from jax.experimental import pallas as pl
from jax.experimental.pallas import tpu as pltpu
from jax.sharding import PartitionSpec as P

HEADS = 8
HEAD = 128
MESH = pl.DeviceIdType.MESH
PARTS = 2


def carried_in(value, axis, join, neutral, backward):
    count, mine = (lax.axis_size(axis), lax.axis_index(axis))
    pieces = lax.all_gather(value, axis)
    if backward:
        pieces = pieces[::-1]
        mine = count - 1 - mine
    running = jnp.full_like(value, 0) + jnp.asarray(neutral, value.dtype)

    def hop(position, running):
        longer = join(running, pieces[position])
        return jnp.where(position < mine, longer, running)

    return lax.fori_loop(0, count - 1, hop, running)


def add_one(earlier, later):
    return earlier + later


def local(query_rows, key_rows, value_rows, out_grad, reg_query, reg_out_grad, reg_offset):
    row_count = query_rows.shape[0]
    reg_count = reg_query.shape[0]
    total_rows = row_count * lax.axis_size("ctx") * lax.axis_size("sub")
    factor = 1.0 / math.sqrt(HEAD * total_rows)
    query_heads = query_rows.reshape(row_count, HEADS, HEAD)
    key_heads = key_rows.reshape(row_count, HEADS, HEAD)
    value_heads = value_rows.reshape(row_count, HEADS, HEAD)
    grad_heads = out_grad.reshape(row_count, HEADS, HEAD)
    regq_heads = reg_query.reshape(reg_count, HEADS, HEAD)
    regg_heads = reg_out_grad.reshape(reg_count, HEADS, HEAD)
    kv_local = jnp.einsum(
        "shd,she->hde", key_heads, value_heads, preferred_element_type=jnp.float32
    )
    grad_local = jnp.einsum(
        "thd,the->hde", query_heads, grad_heads, preferred_element_type=jnp.float32
    ) + jnp.einsum("jhd,jhe->hde", regq_heads, regg_heads, preferred_element_type=jnp.float32)
    every_kv, every_grad = (
        lax.all_gather(kv_local[None], "sub", axis=0, tiled=True),
        lax.all_gather(grad_local[None], "sub", axis=0, tiled=True),
    )
    sub_count = lax.axis_size("sub")
    position = lax.axis_index("sub")
    slots = jnp.arange(sub_count, dtype=jnp.int32)
    earlier_mask = (slots < position)[:, None, None, None]
    later_mask = (slots > position)[:, None, None, None]
    zero_value = jnp.float32(0.0)
    inner_kv = jnp.sum(jnp.where(earlier_mask, every_kv, zero_value), axis=0)
    inner_grad = jnp.sum(jnp.where(later_mask, every_grad, zero_value), axis=0)
    share_rows = kv_local.shape[1] // sub_count
    start_row = position * share_rows
    share_kv = lax.dynamic_slice_in_dim(jnp.sum(every_kv, axis=0), start_row, share_rows, 1)
    share_grad = lax.dynamic_slice_in_dim(jnp.sum(every_grad, axis=0), start_row, share_rows, 1)
    share_zero = jnp.zeros_like(share_kv)
    outer_kv = carried_in(share_kv, "ctx", add_one, share_zero, False)
    outer_grad = carried_in(share_grad, "ctx", add_one, share_zero, True)
    full_kv, full_grad = (
        lax.all_gather(outer_kv, "sub", axis=1, tiled=True),
        lax.all_gather(outer_grad, "sub", axis=1, tiled=True),
    )
    before = (full_kv + inner_kv).astype(jnp.bfloat16)
    after = (full_grad + inner_grad).astype(jnp.bfloat16)
    row_index = jnp.arange(row_count, dtype=jnp.int32)
    causal = row_index[:, None] >= row_index[None, :]
    reg_mask = reg_offset[:, None] >= row_index[None, :]
    zero = jnp.float32(0.0)
    out_scores = jnp.where(
        causal,
        jnp.einsum("the,she->hts", grad_heads, value_heads, preferred_element_type=jnp.float32),
        zero,
    ).astype(jnp.bfloat16)
    qk_scores = jnp.where(
        causal,
        jnp.einsum("thd,shd->hts", query_heads, key_heads, preferred_element_type=jnp.float32),
        zero,
    ).astype(jnp.bfloat16)
    reg_out_scores = jnp.where(
        reg_mask,
        jnp.einsum("jhe,she->hjs", regg_heads, value_heads, preferred_element_type=jnp.float32),
        zero,
    ).astype(jnp.bfloat16)
    reg_qk_scores = jnp.where(
        reg_mask,
        jnp.einsum("jhd,shd->hjs", regq_heads, key_heads, preferred_element_type=jnp.float32),
        zero,
    ).astype(jnp.bfloat16)
    grad_q = jnp.einsum(
        "hts,shd->thd", out_scores, key_heads, preferred_element_type=jnp.float32
    ) + jnp.einsum("the,hde->thd", grad_heads, before, preferred_element_type=jnp.float32)
    grad_rq = jnp.einsum(
        "hjs,shd->jhd", reg_out_scores, key_heads, preferred_element_type=jnp.float32
    ) + jnp.einsum("jhe,hde->jhd", regg_heads, before, preferred_element_type=jnp.float32)
    grad_k = (
        jnp.einsum("hts,thd->shd", out_scores, query_heads, preferred_element_type=jnp.float32)
        + jnp.einsum("hjs,jhd->shd", reg_out_scores, regq_heads, preferred_element_type=jnp.float32)
        + jnp.einsum("she,hde->shd", value_heads, after, preferred_element_type=jnp.float32)
    )
    grad_v = (
        jnp.einsum("hts,the->she", qk_scores, grad_heads, preferred_element_type=jnp.float32)
        + jnp.einsum("hjs,jhe->she", reg_qk_scores, regg_heads, preferred_element_type=jnp.float32)
        + jnp.einsum("shd,hde->she", key_heads, after, preferred_element_type=jnp.float32)
    )
    width = HEADS * HEAD
    return (
        (grad_q * factor).astype(jnp.bfloat16).reshape(row_count, width),
        (grad_k * factor).astype(jnp.bfloat16).reshape(row_count, width),
        (grad_v * factor).astype(jnp.bfloat16).reshape(row_count, width),
        (grad_rq * factor).astype(jnp.bfloat16).reshape(reg_count, width),
    )


def contract(lhs, rhs, lhs_dim, rhs_dim):
    return lax.dot_general(
        lhs, rhs, (((lhs_dim,), (rhs_dim,)), ((), ())), preferred_element_type=jnp.float32
    )


def kernel(
    factor,
    q_hbm, k_hbm, v_hbm, g_hbm, rq_hbm, rg_hbm, off_hbm,
    out_q, out_k, out_v, out_rq,
    off_ref, qa, ga, ka, va, mine, pair, cross_out, cross_in, chain_in, chain_out, other, full, full16,
    acc_q, acc_k, acc_v,
    load_sem, pair_send, pair_recv, cross_send, cross_recv, chain_send, chain_recv,
    own_send, other_send, relay_send, full_recv,
):
    ctx_count, sub_count = lax.axis_size("ctx"), lax.axis_size("sub")
    each = HEADS // sub_count
    units = each * PARTS
    z, s = lax.axis_index("ctx"), lax.axis_index("sub")
    a, c = s // 2, s % 2
    partner = {"sub": 2 * a + 1 - c}
    across = {"sub": 2 * (1 - a) + c}
    rows, regs = ka.shape[0], rq_hbm.shape[0]

    loads = [
        pltpu.make_async_copy(k_hbm, ka, load_sem.at[0]),
        pltpu.make_async_copy(v_hbm, va, load_sem.at[1]),
        pltpu.make_async_copy(q_hbm, qa.at[pl.ds(0, rows)], load_sem.at[2]),
        pltpu.make_async_copy(g_hbm, ga.at[pl.ds(0, rows)], load_sem.at[3]),
        pltpu.make_async_copy(rq_hbm, qa.at[pl.ds(rows, regs)], load_sem.at[4]),
        pltpu.make_async_copy(rg_hbm, ga.at[pl.ds(rows, regs)], load_sem.at[5]),
    ]
    load_offset = pltpu.make_async_copy(off_hbm, off_ref, load_sem.at[6])
    for load in loads:
        load.start()
    load_offset.start()

    barrier = pltpu.get_barrier_semaphore()
    has_prev, has_next = z > 0, z < ctx_count - 1
    for target in (partner, across):
        pl.semaphore_signal(barrier, inc=1, device_id=target, device_id_type=MESH)

    @pl.when(has_prev)
    def _():
        pl.semaphore_signal(barrier, inc=1, device_id={"ctx": z - 1}, device_id_type=MESH)

    @pl.when(has_next)
    def _():
        pl.semaphore_signal(barrier, inc=1, device_id={"ctx": z + 1}, device_id_type=MESH)

    def cols(h):
        return pl.ds(pl.multiple_of(h * HEAD, HEAD), HEAD)

    def whole(h):
        return pl.ds(h * PARTS, PARTS)

    def remote(src, dst, send, recv, target):
        return pltpu.make_async_remote_copy(
            src_ref=src, dst_ref=dst, send_sem=send, recv_sem=recv,
            device_id=target, device_id_type=MESH,
        )

    def pair_copy(k, h):
        return remote(mine.at[k, whole(h)], pair.at[k, whole(h)], pair_send.at[k, h], pair_recv.at[k, h], partner)

    def cross_copy(k, i):
        return remote(
            cross_out.at[k, i], cross_in.at[k, i], cross_send.at[k, i], cross_recv.at[k, i], across
        )

    def chain_copy(k, i, target):
        return remote(
            chain_out.at[k, i], chain_in.at[k, i], chain_send.at[k, i], chain_recv.at[k, i],
            {"ctx": target},
        )

    def own_copy(k, i):
        h = s * units + i
        return remote(full.at[k, h], full.at[k, h], own_send.at[k, i], full_recv.at[k, h], partner)

    def other_copy(k, i):
        return remote(
            other.at[k, i], full.at[k, s * units + i], other_send.at[k, i],
            full_recv.at[k, s * units + i], across,
        )

    def relay_copy(k, i):
        h = across["sub"] * units + i
        return remote(full.at[k, h], full.at[k, h], relay_send.at[k, i], full_recv.at[k, h], partner)

    first = jnp.where(2 * z >= ctx_count, 1, 0)
    kinds = (first, 1 - first)

    def state(h):
        piece = (PARTS, HEAD // PARTS, HEAD)
        mine[0, whole(h)] = contract(ka[:, cols(h)], va[:, cols(h)], 0, 0).reshape(piece)
        mine[1, whole(h)] = contract(qa[:, cols(h)], ga[:, cols(h)], 0, 0).reshape(piece)

    for load in loads:
        load.wait()
    greeted = 2 + jnp.where(has_prev, 1, 0) + jnp.where(has_next, 1, 0)

    for i in range(each):
        state((2 * (1 - a) + 1 - c) * each + i)
    pl.semaphore_wait(barrier, greeted)
    for i in range(each):
        for k in kinds:
            pair_copy(k, (2 * (1 - a) + 1 - c) * each + i).start()
    for i in range(each):
        state(across["sub"] * each + i)
    for k in kinds:
        for i in range(each):
            h = across["sub"] * each + i
            pair_copy(k, h).wait_recv()
            cross_out[k, whole(i)] = mine[k, whole(h)] + pair[k, whole(h)]
            for part in range(PARTS):
                cross_copy(k, i * PARTS + part).start()
    for i in range(each):
        state((2 * a + 1 - c) * each + i)
    for i in range(each):
        for k in kinds:
            pair_copy(k, (2 * a + 1 - c) * each + i).start()
    for i in range(each):
        state(s * each + i)
    for side in range(2):
        for i in range(each):
            pair_copy(c, (2 * side + c) * each + i).start()

    place = lax.broadcasted_iota(jnp.int32, (rows, rows), 0)
    time = lax.broadcasted_iota(jnp.int32, (rows, rows), 1)
    reg_place = lax.broadcasted_iota(jnp.int32, (rows, regs), 0)

    def masked(scores):
        zero = jnp.float32(0.0)
        regular = jnp.where(time >= place, scores[:, :rows], zero)
        register = jnp.where(off_ref[...] >= reg_place, scores[:, rows:], zero)
        return jnp.concatenate([regular, register], axis=1).astype(jnp.bfloat16)

    def scores(h):
        at = cols(h)
        key, value, query, grad = ka[:, at], va[:, at], qa[:, at], ga[:, at]
        out_scores = masked(contract(value, grad, 1, 1))
        qk_scores = masked(contract(key, query, 1, 1))
        acc_q[:, at] = contract(out_scores, key, 0, 0)
        acc_k[:, at] = contract(out_scores, query, 1, 0)
        acc_v[:, at] = contract(qk_scores, grad, 1, 0)

    def some_scores(low, high):
        lax.fori_loop(low, high, lambda h, _: (scores(h), 0)[1], 0)

    def chain(k):
        has_in = jnp.where(k == 0, has_prev, has_next)
        has_out = jnp.where(k == 0, has_next, has_prev)
        target = jnp.where(k == 0, z + 1, z - 1)
        ahead = a == k
        for i in range(each):
            pair_copy(k, s * each + i).wait_recv()
        for i in range(units):
            h = s * units + i
            cross_copy(k, i).wait_recv()

            @pl.when(has_in)
            def _():
                chain_copy(k, i, target).wait_recv()

            @pl.when(jnp.logical_not(has_in))
            def _():
                chain_in[k, i] = jnp.zeros((HEAD // PARTS, HEAD), jnp.float32)

            @pl.when(has_out)
            def _():
                chain_out[k, i] = (chain_in[k, i] + (mine[k, h] + pair[k, h])) + cross_in[k, i]
                chain_copy(k, i, target).start()

            carried = chain_in[k, i]
            zero = jnp.float32(0.0)
            own = mine[k, h] + pair[k, h]
            other[k, i] = carried + jnp.where(ahead, own, zero)
            other_copy(k, i).start()
            full[k, h] = carried + jnp.where(ahead, zero, cross_in[k, i])
            own_copy(k, i).start()

    def relay(k):
        for i in range(units):
            h = across["sub"] * units + i
            remote(
                other.at[k, i], full.at[k, h], other_send.at[k, i], full_recv.at[k, h], across
            ).wait_recv()
            relay_copy(k, i).start()

    def full_wait(h):
        for k in range(2):
            for part in range(PARTS):
                u = h * PARTS + part
                remote(
                    full.at[k, u], full.at[k, u], own_send.at[0, 0], full_recv.at[k, u], partner
                ).wait_recv()

    def finish(h):
        at = cols(h)
        square = (HEAD, HEAD)
        joined = full[1 - c, whole(h)] + pair[1 - c, whole(h)]
        full16[1 - c, h] = joined.reshape(square).astype(jnp.bfloat16)
        full16[c, h] = full[c, whole(h)].reshape(square).astype(jnp.bfloat16)
        before, after = full16[0, h], full16[1, h]
        sums = (acc_q[:, at] + contract(ga[:, at], before, 1, 1)) * factor
        out_q[:, at] = sums[:rows].astype(jnp.bfloat16)
        out_rq[:, at] = sums[rows:].astype(jnp.bfloat16)
        out_k[:, at] = ((acc_k[:, at] + contract(va[:, at], after, 1, 1)) * factor).astype(jnp.bfloat16)
        out_v[:, at] = ((acc_v[:, at] + contract(ka[:, at], after, 1, 0)) * factor).astype(jnp.bfloat16)

    load_offset.wait()
    some_scores(0, 2)
    chain(kinds[0])
    some_scores(2, 4)
    chain(kinds[1])
    relay(kinds[0])
    some_scores(4, HEADS)
    for side in range(2):
        for i in range(each):
            pair_copy(1 - c, (2 * side + 1 - c) * each + i).wait_recv()
    for i in range(each):
        finish(s * each + i)
    for i in range(each):
        h = (2 * a + 1 - c) * each + i
        full_wait(h)
        finish(h)
    relay(kinds[1])
    for i in range(each):
        finish(across["sub"] * each + i)
    for i in range(each):
        h = (2 * (1 - a) + 1 - c) * each + i
        full_wait(h)
        finish(h)

    for k in range(2):
        for i in range(each):
            for side in range(2):
                pair_copy(k, (2 * side + 1 - c) * each + i).wait_send()
        for i in range(units):
            cross_copy(k, i).wait_send()
            other_copy(k, i).wait_send()
            own_copy(k, i).wait_send()
            relay_copy(k, i).wait_send()

            @pl.when((has_next, has_prev)[k])
            def _():
                chain_copy(k, i, (z + 1, z - 1)[k]).wait_send()
    for side in range(2):
        for i in range(each):
            pair_copy(c, (2 * side + c) * each + i).wait_send()


def store_all(*refs):
    copies = [pltpu.make_async_copy(refs[i], refs[4 + i], refs[8].at[i]) for i in range(4)]
    for copy in copies:
        copy.start()
    for copy in copies:
        copy.wait()


def fused(query_rows, key_rows, value_rows, out_grad, reg_query, reg_out_grad, reg_offset):
    rows, width = query_rows.shape
    regs = reg_query.shape[0]
    sub_count = lax.axis_size("sub")
    factor = 1.0 / math.sqrt(HEAD * rows * lax.axis_size("ctx") * sub_count)
    each = HEADS // sub_count
    all_states = pltpu.VMEM((2, HEADS * PARTS, HEAD // PARTS, HEAD), jnp.float32)
    few_states = pltpu.VMEM((2, each * PARTS, HEAD // PARTS, HEAD), jnp.float32)
    all_sems = pltpu.SemaphoreType.DMA((2, HEADS))
    unit_sems = pltpu.SemaphoreType.DMA((2, HEADS * PARTS))
    few_sems = pltpu.SemaphoreType.DMA((2, each * PARTS))
    vmem = pl.BlockSpec(memory_space=pltpu.VMEM)
    hbm = pl.BlockSpec(memory_space=pltpu.HBM)
    shapes = (
        jax.ShapeDtypeStruct((rows, width), jnp.bfloat16),
        jax.ShapeDtypeStruct((rows, width), jnp.bfloat16),
        jax.ShapeDtypeStruct((rows, width), jnp.bfloat16),
        jax.ShapeDtypeStruct((regs, width), jnp.bfloat16),
    )
    results = pl.pallas_call(
        functools.partial(kernel, factor),
        out_shape=shapes,
        in_specs=[hbm] * 7,
        out_specs=(vmem,) * 4,
        scratch_shapes=[
            pltpu.VMEM((1, regs), jnp.int32),
            pltpu.VMEM((rows + regs, width), jnp.bfloat16),
            pltpu.VMEM((rows + regs, width), jnp.bfloat16),
            pltpu.VMEM((rows, width), jnp.bfloat16),
            pltpu.VMEM((rows, width), jnp.bfloat16),
            all_states, all_states,
            few_states, few_states, few_states, few_states, few_states,
            all_states,
            pltpu.VMEM((2, HEADS, HEAD, HEAD), jnp.bfloat16),
            pltpu.VMEM((rows + regs, width), jnp.float32),
            pltpu.VMEM((rows, width), jnp.float32),
            pltpu.VMEM((rows, width), jnp.float32),
            pltpu.SemaphoreType.DMA((7,)),
            all_sems, all_sems,
            few_sems, few_sems, few_sems, few_sems,
            few_sems, few_sems, few_sems, unit_sems,
        ],
        compiler_params=pltpu.CompilerParams(
            collective_id=0, has_side_effects=True, vmem_limit_bytes=40960 * 1024
        ),
    )(
        *[
            pltpu.with_memory_space_constraint(array, pltpu.HBM)
            for array in (query_rows, key_rows, value_rows, out_grad, reg_query, reg_out_grad)
        ],
        pltpu.with_memory_space_constraint(reg_offset.reshape(1, regs), pltpu.HBM),
    )
    return pl.pallas_call(
        store_all,
        out_shape=shapes,
        in_specs=[vmem] * 4,
        out_specs=(hbm,) * 4,
        scratch_shapes=[pltpu.SemaphoreType.DMA((4,))],
        compiler_params=pltpu.CompilerParams(vmem_limit_bytes=1024 * 1024),
    )(*results)


def solution(mesh):
    placed = (
        P(("grp", "ctx", "sub"), None),
        P(("grp", "ctx", "sub"), None),
        P(("grp", "ctx", "sub"), None),
        P(("grp", "ctx", "sub"), None),
        P(("grp", "ctx", "sub"), None),
        P(("grp", "ctx", "sub"), None),
        P(("grp", "ctx", "sub")),
    )
    return jax.shard_map(
        fused if mesh.shape["sub"] == 4 else local,
        mesh=mesh,
        in_specs=placed,
        out_specs=(
            P(("grp", "ctx", "sub"), None),
            P(("grp", "ctx", "sub"), None),
            P(("grp", "ctx", "sub"), None),
            P(("grp", "ctx", "sub"), None),
        ),
        check_vma=False,
    )
```
